128 devices in a mesh: shot: 32 (over x_lo, z, y), freq: 4 (over x_hi, core).
Axes of the slice: x: 4 (x_hi: 2, x_lo: 2; x = x_hi * 2 + x_lo), y: 4, z: 4, core: 2. Of those that a mesh axis runs over, the one named last changes fastest.
Arguments:
- recorded: bfloat16 [2, 256, 2048, 512], P(None, 'freq', 'shot'), may hold values from -6 to 6
- rec_shot: int32 [2048, 512], P('shot'), may hold values from 0 to 2047
- owners: int32 [3], replicated, may hold values from 0 to 31, as said below
Outputs:
- primaries: bfloat16 [2048, 512, 512], P('shot', 'freq')
- filters: float32 [2048, 31], P('shot')
The draws below stay inside these ranges and needn't reach their ends.
Inputs may be any that keep to these rules, and one draw needn't show every extreme that they name: The 3 owners are distinct; the first and the last index of the shot axis are always among them.
All inputs are finite; a program needn't handle non-finite values.
Results may differ from the reference program's by a relative error of at most 0.008.
Values may be sent and summed in bfloat16 or wider, within the bound.
A program may use at most 192 MiB of HBM per device.

```python
import math
import jax
import jax.numpy as jnp
from jax import lax

SHOT_DEV = 64
R = 512
F = 256
TAPS = 31
STEPS = 3
SHOTS = 2048
N_SHOT = 32


def draw_owners(key, part):
    middle_key = jax.random.fold_in(key, 11)
    order_key = jax.random.fold_in(key, 23)
    middle = 1 + jax.random.permutation(middle_key, N_SHOT - 2)[:STEPS - 2]
    chosen = jnp.concatenate([jnp.array([0, N_SHOT - 1], dtype=jnp.int32), middle.astype(jnp.int32)])
    order = jax.random.permutation(order_key, STEPS)
    return chosen[order].astype(jnp.int32)


def with_ends(values, stream_key, low, largest):
    dims = values.shape
    place = [jax.random.randint(jax.random.fold_in(stream_key, axis), (), 0, dims[axis]) for axis in range(len(dims))]
    values = values.at[tuple(place)].set(low)
    longest = dims.index(max(dims))
    place[longest] = (place[longest] + 1) % dims[longest]
    return values.at[tuple(place)].set(largest)


def block_levels(own_key, shape, shards, smallest, high):
    gain, own = 1.0, jax.random.fold_in(own_key, 6)
    for position, parts in shards:
        draws = jnp.exp(jax.random.uniform(jax.random.fold_in(own, position), (parts,), jnp.float32, smallest / len(shards), high / len(shards)))
        gain = gain * jnp.repeat(draws, shape[position] // parts).reshape([-1 if axis == position else 1 for axis in range(len(shape))])
    return gain


def bell_draw(own_key, shape, spread, limit, pieces=(), kind=jnp.bfloat16):
    level = block_levels(own_key, shape, pieces, -0.22, 0.18) if pieces else 1.0
    values = jax.random.normal(own_key, shape, jnp.float32) * spread * level
    return jnp.minimum(jnp.maximum(values, -limit), limit).astype(kind)


def setup_inputs(seed: int = 0) -> dict:
    streams_of = jax.random.split(jax.random.key(seed), 4)
    return {
        "recorded": bell_draw(streams_of[0], (2, F, SHOTS, R), 1.0, 6.0, ((1, 4), (2, 32))),
        "rec_shot": with_ends(jax.random.randint(streams_of[1], (SHOTS, R), 0, SHOTS), jax.random.fold_in(streams_of[1], 1), 0, SHOTS - 1).astype(jnp.int32),
        "owners": draw_owners(jax.random.fold_in(streams_of[3], 71), 0),
    }


REG = 2.0

def angles(freq_index, step_index, period):
    product_mod = jnp.mod(freq_index[:, None] * step_index[None, :], period)
    return product_mod.astype(jnp.float32) * (2.0 * math.pi / period)

def solve_filters(autocorr, crosscorr, tap_count, damping):
    half_taps = (tap_count - 1) // 2
    tap_index = jnp.arange(tap_count, dtype=jnp.int32)
    distance = jnp.abs(tap_index[:, None] - tap_index[None, :])
    normal = autocorr[:, distance] + damping * jnp.eye(tap_count, dtype=jnp.float32)[None, :, :]
    target = crosscorr + damping * (tap_index == half_taps).astype(jnp.float32)[None, :]
    factor = jnp.linalg.cholesky(normal)
    middle = lax.linalg.triangular_solve(factor, target[:, :, None], left_side=True, lower=True)
    solved = lax.linalg.triangular_solve(factor, middle, left_side=True, lower=True, transpose_a=True)
    return solved[:, :, 0]

def band_table(freq_index, freq_count):
    period = 2 * freq_count
    phase_angles = angles(freq_index, jnp.arange(period, dtype=jnp.int32), period)
    norm_factor = 1.0 / math.sqrt(freq_count)
    return jnp.stack([jnp.cos(phase_angles) * norm_factor, -jnp.sin(phase_angles) * norm_factor]).astype(jnp.bfloat16)

def reference(recorded, rec_shot, owners):
    shot_total = recorded.shape[2]
    recv_count = recorded.shape[3]
    half_taps = (TAPS - 1) // 2
    pred_gain = (N_SHOT / (2.0 * recv_count * STEPS)) ** 0.5
    shot_rows = jnp.arange(shot_total, dtype=jnp.int32)[:, None]

    def predict(freq_slab):
        summed = jnp.zeros((2, shot_total, recv_count), jnp.float32)
        for step_index in range(STEPS):
            first_shot = (owners[step_index] * SHOT_DEV).astype(jnp.int32)
            owner_block = lax.dynamic_slice_in_dim(freq_slab, first_shot, SHOT_DEV, 1)
            offset_index = rec_shot - first_shot
            inside = (offset_index >= 0) & (offset_index < SHOT_DEV)
            column = jnp.where(inside, offset_index, SHOT_DEV).astype(jnp.int32)
            binned = jnp.zeros((2, shot_total, SHOT_DEV + 1), jnp.float32)
            binned = binned.at[:, shot_rows, column].add(freq_slab.astype(jnp.float32))
            coeffs = binned[:, :, :SHOT_DEV].astype(jnp.bfloat16)
            real_part = jnp.dot(coeffs[0].astype(jnp.float32), owner_block[0].astype(jnp.float32), preferred_element_type=jnp.float32) - jnp.dot(coeffs[1].astype(jnp.float32), owner_block[1].astype(jnp.float32), preferred_element_type=jnp.float32)
            imag_part = jnp.dot(coeffs[0].astype(jnp.float32), owner_block[1].astype(jnp.float32), preferred_element_type=jnp.float32) + jnp.dot(coeffs[1].astype(jnp.float32), owner_block[0].astype(jnp.float32), preferred_element_type=jnp.float32)
            summed = summed + jnp.stack([real_part, imag_part])
        predicted = (pred_gain * summed).astype(jnp.bfloat16)
        pred_wide = predicted.astype(jnp.float32)
        data_wide = freq_slab.astype(jnp.float32)
        spectrum = lax.optimization_barrier(jnp.sum(pred_wide[0] * pred_wide[0] + pred_wide[1] * pred_wide[1], axis=1))
        cross_real = lax.optimization_barrier(jnp.sum(pred_wide[0] * data_wide[0] + pred_wide[1] * data_wide[1], axis=1))
        cross_imag = lax.optimization_barrier(jnp.sum(pred_wide[0] * data_wide[1] - pred_wide[1] * data_wide[0], axis=1))
        return (predicted, spectrum, cross_real, cross_imag)
    predicted, spectrum, cross_real, cross_imag = lax.map(predict, jnp.swapaxes(recorded, 0, 1))
    highest = lax.Precision.HIGHEST
    freq_index = jnp.arange(F, dtype=jnp.int32)
    tap_index = jnp.arange(TAPS, dtype=jnp.int32)
    lag_angles = angles(freq_index, tap_index, 2 * F)
    tap_angles = angles(freq_index, tap_index - half_taps, 2 * F)
    autocorr = jnp.dot(spectrum.T, jnp.cos(lag_angles), precision=highest)
    crosscorr = jnp.dot(cross_real.T, jnp.cos(tap_angles), precision=highest) - jnp.dot(cross_imag.T, jnp.sin(tap_angles), precision=highest)
    filters = solve_filters(autocorr, crosscorr, TAPS, REG * recv_count * F)
    resp_real = jnp.dot(jnp.cos(tap_angles), filters.T, precision=highest)
    resp_imag = -jnp.dot(jnp.sin(tap_angles), filters.T, precision=highest)
    full_table = band_table(freq_index, F).reshape(2 * F, 2 * F)
    outputs = []
    for block_index in range(N_SHOT):
        shot_begin = block_index * SHOT_DEV
        shot_end = shot_begin + SHOT_DEV
        pred_block = predicted[:, :, shot_begin:shot_end].astype(jnp.float32)
        data_block = recorded[:, :, shot_begin:shot_end].astype(jnp.float32)
        real_resp = resp_real[:, shot_begin:shot_end, None]
        imag_resp = resp_imag[:, shot_begin:shot_end, None]
        res_real = data_block[0] - (real_resp * pred_block[:, 0] - imag_resp * pred_block[:, 1])
        res_imag = data_block[1] - (real_resp * pred_block[:, 1] + imag_resp * pred_block[:, 0])
        residual = jnp.stack([res_real, res_imag]).astype(jnp.bfloat16)
        flattened = residual.reshape(2 * F, SHOT_DEV * recv_count)
        time_rows = jnp.dot(flattened.T.astype(jnp.float32), full_table.astype(jnp.float32), preferred_element_type=jnp.float32)
        outputs.append(time_rows.reshape(SHOT_DEV, recv_count, 2 * F).astype(jnp.bfloat16))
    return (jnp.concatenate(outputs, axis=0), filters)
```

```python
import math

import jax
import jax.numpy as jnp
import numpy as np
from jax import lax
from jax.experimental import pallas as pl
from jax.experimental.pallas import tpu as pltpu
from jax.sharding import PartitionSpec as P

F = 256
TAPS = 31
STEPS = 3
HALF = (TAPS - 1) // 2
REG = 2.0
N_SHOT = 32
N_FREQ = 4
N_DEV = N_SHOT * N_FREQ
FL = F // N_DEV
SD = 64
R = 512
BLK = 16
MIB = 1 << 20
LIMIT = 60 * MIB
WINDOW = 8
HIGH = lax.Precision.HIGHEST
MESH = pl.DeviceIdType.MESH


def device_freqs():
    dev = np.arange(N_DEV)
    return (dev % N_FREQ)[:, None] * (F // N_FREQ) + (dev // N_FREQ)[:, None] * FL + np.arange(FL)[None, :]


def angle(freq, step):
    return ((freq * step) % (2 * F)).astype(np.float64) * (2.0 * math.pi / (2 * F))


def corr_table():
    freqs = device_freqs().reshape(N_SHOT, N_FREQ, FL)
    lags = np.abs(np.arange(64) - (TAPS - 1))
    taps = np.arange(32) - HALF
    table = np.zeros((N_FREQ, 96, N_SHOT, 8))
    for j in range(FL):
        col = freqs[:, :, j].T[:, None, :]
        table[:, :64, :, 3 * j] = np.cos(angle(col, lags[None, :, None]))
        table[:, 64:, :, 3 * j + 1] = np.cos(angle(col, taps[None, :, None]))
        table[:, 64:, :, 3 * j + 2] = -np.sin(angle(col, taps[None, :, None]))
    return table.reshape(N_FREQ, 96, N_SHOT * 8).astype(np.float32)


def resp_table():
    freqs = device_freqs().reshape(N_SHOT, N_FREQ, FL)
    taps = np.arange(32) - HALF
    valid = np.arange(32) < TAPS
    table = np.zeros((N_FREQ, N_SHOT, 8, 32))
    for j in range(FL):
        ang = angle(freqs[:, :, j].T[:, :, None], taps[None, None, :])
        table[:, :, j] = np.cos(ang) * valid
        table[:, :, FL + j] = -np.sin(ang) * valid
    return table.reshape(N_FREQ, N_SHOT * 8, 32).astype(np.float32)


def time_table():
    freqs = device_freqs()
    ang = angle(freqs[:, :, None], np.arange(2 * F)[None, None, :])
    norm = 1.0 / math.sqrt(F)
    table = np.stack([np.cos(ang) * norm, -np.sin(ang) * norm], axis=1)
    return table.reshape(2 * F, 2 * F).astype(np.float32)


def predict_kernel(gain, owners_ref, c_ref, x_ref, oa_ref, ob_ref, oc_ref, pred_ref, corr_ref, w_ref):
    @pl.when(pl.program_id(0) == 0)
    def _():
        for j in range(FL):
            for t, o_ref in enumerate((oa_ref, ob_ref, oc_ref)):
                real, imag = o_ref[0, 0, j], o_ref[0, 1, j]
                top = slice(t * SD, (t + 1) * SD)
                under = 3 if t == 2 else 4 + t
                low = slice(under * SD, (under + 1) * SD)
                w_ref[j, top, :R] = real
                w_ref[j, top, R:] = imag
                w_ref[j, low, :R] = -imag
                w_ref[j, low, R:] = real

    n = c_ref.shape[0]
    rows = n * SD
    lane = lax.broadcasted_iota(jnp.int32, (rows, 128), 1)
    cols = jnp.zeros((rows, 128), jnp.float32)
    for j in range(FL):
        lhs = c_ref[:, j].reshape(rows, 2 * STEPS * SD)
        acc = jnp.dot(lhs, w_ref[j], preferred_element_type=jnp.float32)
        pred = (gain * acc).astype(jnp.bfloat16)
        pr, pi = pred[:, :R], pred[:, R:]
        pred_ref[:, 0, j] = pr.reshape(n, SD, R)
        pred_ref[:, 1, j] = pi.reshape(n, SD, R)
        pr, pi = pr.astype(jnp.float32), pi.astype(jnp.float32)
        xr = x_ref[:, 0, j].reshape(rows, R).astype(jnp.float32)
        xi = x_ref[:, 1, j].reshape(rows, R).astype(jnp.float32)
        spec = jnp.sum(pr * pr + pi * pi, axis=1, keepdims=True)
        cr = jnp.sum(pr * xr + pi * xi, axis=1, keepdims=True)
        ci = jnp.sum(pr * xi - pi * xr, axis=1, keepdims=True)
        for q, col in enumerate((spec, cr, ci)):
            cols = jnp.where(lane == 3 * j + q, col, cols)
    flat = cols.T[:8]
    for m in range(n):
        pair = flat[:, (m // 2) * 128 : (m // 2) * 128 + 128]
        corr_ref[m] = pair if m % 2 == 0 else pltpu.roll(pair, SD, 1)


def predict(owners, coeffs, data, gain):
    step = 4
    grid = N_SHOT // step
    owner_spec = [
        pl.BlockSpec((1, 2, FL, SD, R), lambda i, ow, t=t: (ow[t], 0, 0, 0, 0)) for t in range(STEPS)
    ]
    return pl.pallas_call(
        lambda *refs: predict_kernel(gain, *refs),
        grid_spec=pltpu.PrefetchScalarGridSpec(
            num_scalar_prefetch=1,
            grid=(grid,),
            in_specs=[
                pl.BlockSpec((step, FL, SD, 2 * STEPS * SD), lambda i, ow: (i, 0, 0, 0)),
                pl.BlockSpec((step, 2, FL, SD, R), lambda i, ow: (i, 0, 0, 0, 0)),
            ]
            + owner_spec,
            out_specs=[
                pl.BlockSpec((step, 2, FL, SD, R), lambda i, ow: (i, 0, 0, 0, 0)),
                pl.BlockSpec((step, 8, 128), lambda i, ow: (i, 0, 0)),
            ],
            scratch_shapes=[pltpu.VMEM((FL, 2 * STEPS * SD, 2 * R), jnp.bfloat16)],
        ),
        out_shape=(
            jax.ShapeDtypeStruct(data.shape, jnp.bfloat16),
            jax.ShapeDtypeStruct((N_SHOT, 8, 128), jnp.float32),
        ),
        compiler_params=pltpu.CompilerParams(
            dimension_semantics=("arbitrary",), vmem_limit_bytes=LIMIT
        ),
        cost_estimate=pl.CostEstimate(flops=4 * 10**9, bytes_accessed=28 * 10**6, transcendentals=0),
        name="predict",
    )(owners, coeffs, data, data, data, data)


def signed(flip, offset, size):
    return jnp.where(flip == 1, lax.rem(size - offset, size), offset)


def shot_peer_of(me, me_freq, n):
    x, z, y = me // 16, lax.rem(me // 4, 4), lax.rem(me, 4)
    flip = lax.rem(lax.rem(me_freq, 2) + x + y + z, 2)
    d = lax.rem(n * 11, N_SHOT)
    x = lax.rem(x + d // 16, 2)
    z = lax.rem(z + signed(flip, lax.rem(d // 4, 4), 4), 4)
    y = lax.rem(y + signed(flip, lax.rem(d, 4), 4), 4)
    return x * 16 + z * 4 + y


def any_peer_of(me, me_freq, n):
    core = lax.rem(me_freq, 2)
    d = lax.rem(n * 43, N_DEV)
    x = lax.rem((me_freq // 2) * 2 + me // 16 + signed(core, lax.rem(d // 16, 4), 4), 4)
    z = lax.rem(lax.rem(me // 4, 4) + signed(core, lax.rem(d // 4, 4), 4), 4)
    y = lax.rem(lax.rem(me, 4) + signed(core, lax.rem(d, 4), 4), 4)
    other = lax.rem(core + d // 64, 2)
    return lax.rem(x, 2) * 16 + z * 4 + y, (x // 2) * 2 + other


def greet(me, me_freq, with_freq, with_all):
    barrier = pltpu.get_barrier_semaphore()

    def shot_peer(n, carry):
        peer = shot_peer_of(me, me_freq, n)
        pl.semaphore_signal(barrier, 1, device_id=(peer, me_freq), device_id_type=MESH)
        return carry

    def any_peer(n, carry):
        pl.semaphore_signal(barrier, 1, device_id=any_peer_of(me, me_freq, n), device_id_type=MESH)
        return carry

    if with_all:
        lax.fori_loop(1, N_DEV, any_peer, 0)
        pl.semaphore_wait(barrier, N_DEV - 1)
        return
    lax.fori_loop(1, N_SHOT, shot_peer, 0)
    count = N_SHOT - 1
    if with_freq:
        for e in range(1, N_FREQ):
            pl.semaphore_signal(
                barrier, 1, device_id=(me, lax.rem(me_freq + e, N_FREQ)), device_id_type=MESH
            )
        count += N_FREQ - 1
    pl.semaphore_wait(barrier, count)


def exchange_kernel(
    owners_ref, rec_ref, shot_ref, x_ref, c_ref,
    block, wide, narrow, coeffs, load_sem, own_sem, send_sem, recv_sem, csend_sem, crecv_sem,
):
    me = lax.axis_index("shot")
    me_freq = lax.axis_index("freq")
    freqs = rec_ref.shape[1]
    rows = 2 * freqs

    def load(b):
        return pltpu.make_async_copy(
            rec_ref.at[:, :, pl.ds(b * BLK, BLK), :], block.at[b % 2], load_sem.at[b % 2]
        )

    def data_copy(d):
        peer = shot_peer_of(me, me_freq, d)
        return pltpu.make_async_remote_copy(
            src_ref=rec_ref.at[:, pl.ds(peer * FL, FL)],
            dst_ref=x_ref.at[me],
            send_sem=send_sem.at[d],
            recv_sem=recv_sem.at[d],
            device_id=(peer, me_freq),
            device_id_type=MESH,
        )

    def coeff_copy(d):
        peer = shot_peer_of(me, me_freq, d)
        return pltpu.make_async_remote_copy(
            src_ref=coeffs.at[pl.ds(peer * FL, FL)],
            dst_ref=c_ref.at[me],
            send_sem=csend_sem.at[d],
            recv_sem=crecv_sem.at[d],
            device_id=(peer, me_freq),
            device_id_type=MESH,
        )

    def run(action):
        def body(d, carry):
            action(d)
            return carry

        lax.fori_loop(1, N_SHOT, body, 0)

    def send_next(copy, d):
        copy(d - WINDOW).wait_send()
        copy(d).start()

    load(0).start()
    greet(me, me_freq, False, False)
    for d in range(1, WINDOW + 1):
        data_copy(d).start()
    own = pltpu.make_async_copy(rec_ref.at[:, pl.ds(me * FL, FL)], x_ref.at[me], own_sem.at[0])
    own.start()

    slot = lax.broadcasted_iota(jnp.int32, (4 * SD, R), 0)
    key = jnp.where(slot < SD, owners_ref[0] * SD + slot, owners_ref[1] * SD + slot - SD)
    key = jnp.where(slot < 2 * SD, key, owners_ref[2] * SD + slot - 2 * SD)
    key = jnp.where(slot < 3 * SD, key, -1)
    for b in range(SD // BLK):
        if b + 1 < SD // BLK:
            load(b + 1).start()
        load(b).wait()
        for ch in range(R // 128):
            part = block[b % 2, :, :, :, ch * 128 : (ch + 1) * 128]
            wide[ch] = part.astype(jnp.float32).reshape(rows * BLK, 128)

        def bin_shot(m, carry):
            data = jnp.concatenate(
                [wide[ch, pl.ds(m, rows, stride=BLK), :] for ch in range(R // 128)], axis=1
            ).astype(jnp.bfloat16)
            where = shot_ref[pl.ds(b * BLK + m, 1), :]
            one_hot = (jnp.broadcast_to(where, key.shape) == key).astype(jnp.bfloat16)
            out = lax.dot_general(
                data, one_hot, (((1,), (1,)), ((), ())), preferred_element_type=jnp.float32
            )
            real, imag = out[:freqs], out[freqs:]
            narrow[0, pl.ds(m, freqs, stride=BLK), :] = real[:, :128]
            narrow[1, pl.ds(m, freqs, stride=BLK), :] = real[:, 128:] + pltpu.roll(imag[:, 128:], SD, 1)
            narrow[2, pl.ds(m, freqs, stride=BLK), :] = imag[:, :128]
            due = b * BLK + m

            @pl.when((lax.rem(due, 2) == 0) & (due // 2 + WINDOW + 1 < N_SHOT))
            def _():
                send_next(data_copy, due // 2 + WINDOW + 1)

            return carry

        lax.fori_loop(0, BLK, bin_shot, 0)
        for ch in range(3):
            part = narrow[ch].reshape(freqs, BLK, 128).astype(jnp.bfloat16)
            coeffs[:, b * BLK : (b + 1) * BLK, ch * 128 : (ch + 1) * 128] = part
    mine = pltpu.make_async_copy(coeffs.at[pl.ds(me * FL, FL)], c_ref.at[me], own_sem.at[1])
    mine.start()

    def data_to_coeff(d, carry):
        data_copy(N_SHOT - 1 - WINDOW + d).wait_send()
        coeff_copy(d).start()
        return carry

    def coeff_step(d, carry):
        send_next(coeff_copy, d)
        return carry

    def coeff_end(d, carry):
        coeff_copy(d).wait_send()
        return carry

    lax.fori_loop(1, WINDOW + 1, data_to_coeff, 0)
    lax.fori_loop(WINDOW + 1, N_SHOT, coeff_step, 0)
    lax.fori_loop(N_SHOT - WINDOW, N_SHOT, coeff_end, 0)
    own.wait()
    mine.wait()
    run(lambda d: data_copy(d).wait_recv())
    run(lambda d: coeff_copy(d).wait_recv())


def exchange(owners, recorded, rec_shot):
    freqs = recorded.shape[1]
    width = 2 * STEPS * SD
    anywhere = pl.BlockSpec(memory_space=pl.ANY)
    return pl.pallas_call(
        exchange_kernel,
        in_specs=[
            pl.BlockSpec(memory_space=pltpu.SMEM),
            anywhere,
            pl.BlockSpec(memory_space=pltpu.VMEM),
        ],
        out_specs=[anywhere, anywhere],
        out_shape=(
            jax.ShapeDtypeStruct((N_SHOT, 2, FL, SD, R), jnp.bfloat16),
            jax.ShapeDtypeStruct((N_SHOT, FL, SD, width), jnp.bfloat16),
        ),
        scratch_shapes=[
            pltpu.VMEM((2, 2, freqs, BLK, R), jnp.bfloat16),
            pltpu.VMEM((R // 128, 2 * freqs * BLK, 128), jnp.float32),
            pltpu.VMEM((3, freqs * BLK, 128), jnp.float32),
            pltpu.VMEM((freqs, SD, width), jnp.bfloat16),
            pltpu.SemaphoreType.DMA((2,)),
            pltpu.SemaphoreType.DMA((2,)),
            pltpu.SemaphoreType.DMA((N_SHOT,)),
            pltpu.SemaphoreType.DMA((N_SHOT,)),
            pltpu.SemaphoreType.DMA((N_SHOT,)),
            pltpu.SemaphoreType.DMA((N_SHOT,)),
        ],
        compiler_params=pltpu.CompilerParams(
            collective_id=0, has_side_effects=True, vmem_limit_bytes=LIMIT
        ),
        name="exchange",
    )(owners, recorded, rec_shot)


def filter_kernel(
    damping, corr_ref, ct_ref, rt_ref, filt_ref, resp_ref,
    arrived, parts, answer, ext_ref, send_sem, recv_sem, fsend_sem, frecv_sem, rsend_sem, rrecv_sem,
):
    me = lax.axis_index("shot")
    me_freq = lax.axis_index("freq")

    def corr_copy(d):
        peer = shot_peer_of(me, me_freq, d)
        return pltpu.make_async_remote_copy(
            src_ref=corr_ref.at[peer],
            dst_ref=arrived.at[me],
            send_sem=send_sem.at[d],
            recv_sem=recv_sem.at[d],
            device_id=(peer, me_freq),
            device_id_type=MESH,
        )

    def part_copy(e):
        return pltpu.make_async_remote_copy(
            src_ref=parts.at[me_freq],
            dst_ref=parts.at[me_freq],
            send_sem=fsend_sem.at[e],
            recv_sem=frecv_sem.at[e],
            device_id=(me, lax.rem(me_freq + e, N_FREQ)),
            device_id_type=MESH,
        )

    def resp_copy(d):
        peer = shot_peer_of(me, me_freq, d)
        return pltpu.make_async_remote_copy(
            src_ref=answer.at[peer],
            dst_ref=resp_ref.at[me],
            send_sem=rsend_sem.at[d],
            recv_sem=rrecv_sem.at[d],
            device_id=(peer, me_freq),
            device_id_type=MESH,
        )

    def run(action):
        def body(d, carry):
            action(d)
            return carry

        lax.fori_loop(1, N_SHOT, body, 0)

    greet(me, me_freq, True, False)
    run(lambda d: corr_copy(d).start())
    arrived[me] = corr_ref[me]
    run(lambda d: corr_copy(d).wait())
    parts[me_freq] = jnp.dot(
        ct_ref[...],
        arrived[...].reshape(N_SHOT * 8, 128),
        precision=HIGH,
        preferred_element_type=jnp.float32,
    )
    for e in range(1, N_FREQ):
        part_copy(e).start()
    for e in range(1, N_FREQ):
        part_copy(e).wait()
    total = parts[0]
    for e in range(1, N_FREQ):
        total = total + parts[e]

    row64 = lax.broadcasted_iota(jnp.int32, (64, 128), 0)
    row = lax.broadcasted_iota(jnp.int32, (32, 128), 0)
    ext_ref[...] = total[:64] + jnp.where(row64 == TAPS - 1, damping, 0.0)
    rhs = total[64:] + jnp.where(row == HALF, damping, 0.0)
    cols = [ext_ref[pl.ds(TAPS - 1 - k, 32), :] for k in range(TAPS)]
    inverse = []
    for p in range(TAPS):
        inv = 1.0 / cols[p][p : p + 1, :]
        inverse.append(inv)
        if p == TAPS - 1:
            break
        factor = jnp.where(row > p, cols[p] * inv, 0.0)
        rhs = rhs - factor * rhs[p : p + 1, :]
        for k in range(p + 1, TAPS):
            cols[k] = cols[k] - factor * cols[k][p : p + 1, :]
    found = jnp.zeros((32, 128), jnp.float32)
    for p in range(TAPS - 1, -1, -1):
        value = rhs[p : p + 1, :] * inverse[p]
        found = jnp.where(row == p, value, found)
        rhs = rhs - cols[p] * value
    resp = jnp.dot(rt_ref[...], found, precision=HIGH, preferred_element_type=jnp.float32)
    answer[...] = resp.reshape(N_SHOT, 8, 128)
    run(lambda d: resp_copy(d).start())
    resp_ref[me] = answer[me]
    filt_ref[...] = jnp.concatenate([found, jnp.zeros((96, 128), jnp.float32)], axis=0).T[:SD]
    run(lambda d: resp_copy(d).wait())


def match(corr, ct, rt, damping):
    return pl.pallas_call(
        lambda *refs: filter_kernel(damping, *refs),
        in_specs=[pl.BlockSpec(memory_space=pltpu.VMEM)] * 3,
        out_specs=[pl.BlockSpec(memory_space=pltpu.VMEM)] * 2,
        out_shape=(
            jax.ShapeDtypeStruct((SD, 128), jnp.float32),
            jax.ShapeDtypeStruct((N_SHOT, 8, 128), jnp.float32),
        ),
        scratch_shapes=[
            pltpu.VMEM((N_SHOT, 8, 128), jnp.float32),
            pltpu.VMEM((N_FREQ, 96, 128), jnp.float32),
            pltpu.VMEM((N_SHOT, 8, 128), jnp.float32),
            pltpu.VMEM((64, 128), jnp.float32),
            pltpu.SemaphoreType.DMA((N_SHOT,)),
            pltpu.SemaphoreType.DMA((N_SHOT,)),
            pltpu.SemaphoreType.DMA((N_FREQ,)),
            pltpu.SemaphoreType.DMA((N_FREQ,)),
            pltpu.SemaphoreType.DMA((N_SHOT,)),
            pltpu.SemaphoreType.DMA((N_SHOT,)),
        ],
        compiler_params=pltpu.CompilerParams(
            collective_id=1, has_side_effects=True, vmem_limit_bytes=16 * MIB
        ),
        name="match",
    )(corr, ct, rt)


def residual_kernel(
    x_ref, p_ref, resp_ref, out_ref, xb, pb, sb, load_sem, own_sem, send_sem, recv_sem
):
    me = lax.axis_index("shot")
    me_freq = lax.axis_index("freq")
    mine = me * N_FREQ + me_freq
    width = R // N_FREQ
    diagonal = lax.broadcasted_iota(jnp.int32, (SD, 128), 0) == lax.broadcasted_iota(
        jnp.int32, (SD, 128), 1
    )
    load_x = pltpu.make_async_copy(x_ref, xb, load_sem.at[0])
    load_p = pltpu.make_async_copy(p_ref, pb, load_sem.at[1])

    def copy(n):
        return pltpu.make_async_remote_copy(
            src_ref=sb.at[n],
            dst_ref=out_ref.at[mine],
            send_sem=send_sem.at[n],
            recv_sem=recv_sem.at[n],
            device_id=any_peer_of(me, me_freq, n),
            device_id_type=MESH,
        )

    def compute(n):
        shot, freq = any_peer_of(me, me_freq, n)
        resp = resp_ref[shot]
        part = pl.ds(pl.multiple_of(freq * width, width), width)

        def column(q):
            spread = jnp.broadcast_to(resp[q : q + 1], (SD, 128))
            return jnp.sum(jnp.where(diagonal, spread, 0.0), axis=1, keepdims=True)

        for j in range(FL):
            real, imag = column(j), column(FL + j)
            xr = xb[shot, 0, j, :, part].astype(jnp.float32)
            xi = xb[shot, 1, j, :, part].astype(jnp.float32)
            pr = pb[shot, 0, j, :, part].astype(jnp.float32)
            pi = pb[shot, 1, j, :, part].astype(jnp.float32)
            sb[n, 0, j] = (xr - (real * pr - imag * pi)).astype(jnp.bfloat16)
            sb[n, 1, j] = (xi - (real * pi + imag * pr)).astype(jnp.bfloat16)

    load_x.start()
    load_p.start()
    greet(me, me_freq, False, True)
    load_x.wait()
    load_p.wait()

    def step(n, carry):
        compute(n)
        copy(n).start()
        return carry

    lax.fori_loop(1, N_DEV, step, 0)
    compute(0)
    own = pltpu.make_async_copy(sb.at[0], out_ref.at[mine], own_sem.at[0])
    own.start()
    own.wait()

    def finish(n, carry):
        copy(n).wait()
        return carry

    lax.fori_loop(1, N_DEV, finish, 0)


def residual(data, pred, resp):
    width = R // N_FREQ
    anywhere = pl.BlockSpec(memory_space=pl.ANY)
    return pl.pallas_call(
        residual_kernel,
        in_specs=[anywhere, anywhere, pl.BlockSpec(memory_space=pltpu.VMEM)],
        out_specs=anywhere,
        out_shape=jax.ShapeDtypeStruct((N_DEV, 2, FL, SD, width), jnp.bfloat16),
        scratch_shapes=[
            pltpu.VMEM((N_SHOT, 2, FL, SD, R), jnp.bfloat16),
            pltpu.VMEM((N_SHOT, 2, FL, SD, R), jnp.bfloat16),
            pltpu.VMEM((N_DEV, 2, FL, SD, width), jnp.bfloat16),
            pltpu.SemaphoreType.DMA((2,)),
            pltpu.SemaphoreType.DMA((1,)),
            pltpu.SemaphoreType.DMA((N_DEV,)),
            pltpu.SemaphoreType.DMA((N_DEV,)),
        ],
        compiler_params=pltpu.CompilerParams(
            collective_id=2, has_side_effects=True, vmem_limit_bytes=LIMIT
        ),
        name="residual",
    )(data, pred, resp)


def transform_kernel(r_ref, t_ref, *rest):
    out_ref, wide_ref = rest[-2:]
    k = r_ref.shape[0]
    s = r_ref.shape[1]
    wide_ref[...] = r_ref[...].astype(jnp.float32).reshape(k * s, 128)
    group = 4
    for m in range(0, s, group):
        rows = jnp.concatenate(
            [wide_ref[pl.ds(m + g, k, stride=s), :].T.astype(jnp.bfloat16) for g in range(group)], axis=0
        )
        out = jnp.dot(rows, t_ref[...], preferred_element_type=jnp.float32).astype(jnp.bfloat16)
        out_ref[m : m + group] = out.reshape(group, 128, 2 * F)


def transform(spectra, table, chunk, before):
    k, shots, recv = spectra.shape
    step = 16
    base = chunk * (shots // step)
    in_specs = [
        pl.BlockSpec((k, step, recv), lambda i: (0, i, 0)),
        pl.BlockSpec((k, 2 * F), lambda i: (0, 0)),
    ]
    args = [spectra, table]
    alias = {}
    if before is not None:
        in_specs.append(pl.BlockSpec(memory_space=pl.ANY))
        args.append(before)
        alias = {2: 0}
    return pl.pallas_call(
        transform_kernel,
        grid=(shots // step,),
        in_specs=in_specs,
        out_specs=pl.BlockSpec((step, recv, 2 * F), lambda i: (i + base, 0, 0)),
        out_shape=jax.ShapeDtypeStruct((SD, recv, 2 * F), jnp.bfloat16),
        scratch_shapes=[pltpu.VMEM((k * step, recv), jnp.float32)],
        input_output_aliases=alias,
        compiler_params=pltpu.CompilerParams(
            dimension_semantics=("arbitrary",), vmem_limit_bytes=LIMIT
        ),
        cost_estimate=pl.CostEstimate(flops=2 * 10**9, bytes_accessed=12 * 10**6, transcendentals=0),
        name=f"transform{chunk}",
    )(*args)


def per_device(recorded, rec_shot, owners):
    gain = (N_SHOT / (2.0 * R * STEPS)) ** 0.5
    me_freq = lax.axis_index("freq")
    ct = lax.dynamic_index_in_dim(jnp.asarray(corr_table()), me_freq, 0, False)
    rt = lax.dynamic_index_in_dim(jnp.asarray(resp_table()), me_freq, 0, False)
    data, coeffs = exchange(owners, recorded, rec_shot)
    pred, corr = predict(owners, coeffs, data, gain)
    filt, resp = match(corr, ct, rt, REG * R * F)
    res = residual(data, pred, resp)
    table = jnp.asarray(time_table(), dtype=jnp.bfloat16)
    primaries = transform(res.reshape(2 * F, SD, R // N_FREQ), table, 0, None)
    return (primaries, filt[:, :TAPS])


def solution(mesh):
    placed = (P(None, "freq", "shot", None), P("shot", None), P())
    return jax.shard_map(
        per_device,
        mesh=mesh,
        in_specs=placed,
        out_specs=(P("shot", "freq", None), P("shot", None)),
        check_vma=False,
    )
```

```python
import math

import jax
import jax.numpy as jnp
import numpy as np
from jax import lax
from jax.experimental import pallas as pl
from jax.experimental.pallas import tpu as pltpu
from jax.sharding import PartitionSpec as P

F = 256
TAPS = 31
STEPS = 3
HALF = (TAPS - 1) // 2
REG = 2.0
N_SHOT = 32
N_FREQ = 4
N_DEV = N_SHOT * N_FREQ
FL = F // N_DEV
SD = 64
R = 512
BLK = 16
MIB = 1 << 20
LIMIT = 60 * MIB
GROUP = 4
WINDOW = 8
HIGH = lax.Precision.HIGHEST
MESH = pl.DeviceIdType.MESH


def device_freqs():
    dev = np.arange(N_DEV)
    return (dev % N_FREQ)[:, None] * (F // N_FREQ) + (dev // N_FREQ)[:, None] * FL + np.arange(FL)[None, :]


def angle(freq, step):
    return ((freq * step) % (2 * F)).astype(np.float64) * (2.0 * math.pi / (2 * F))


def corr_table():
    freqs = device_freqs().reshape(N_SHOT, N_FREQ, FL)
    lags = np.abs(np.arange(64) - (TAPS - 1))
    taps = np.arange(32) - HALF
    table = np.zeros((N_FREQ, 96, N_SHOT, 8))
    for j in range(FL):
        col = freqs[:, :, j].T[:, None, :]
        table[:, :64, :, 3 * j] = np.cos(angle(col, lags[None, :, None]))
        table[:, 64:, :, 3 * j + 1] = np.cos(angle(col, taps[None, :, None]))
        table[:, 64:, :, 3 * j + 2] = -np.sin(angle(col, taps[None, :, None]))
    return table.reshape(N_FREQ, 96, N_SHOT * 8).astype(np.float32)


def resp_table():
    freqs = device_freqs().reshape(N_SHOT, N_FREQ, FL)
    taps = np.arange(32) - HALF
    valid = np.arange(32) < TAPS
    table = np.zeros((N_FREQ, N_SHOT, 8, 32))
    for j in range(FL):
        ang = angle(freqs[:, :, j].T[:, :, None], taps[None, None, :])
        table[:, :, j] = np.cos(ang) * valid
        table[:, :, FL + j] = -np.sin(ang) * valid
    return table.reshape(N_FREQ, N_SHOT * 8, 32).astype(np.float32)


def time_table():
    freqs = device_freqs()
    ang = angle(freqs[:, :, None], np.arange(2 * F)[None, None, :])
    norm = 1.0 / math.sqrt(F)
    table = np.stack([np.cos(ang) * norm, -np.sin(ang) * norm], axis=1)
    return table.reshape(2 * F, 2 * F).astype(np.float32)


def turned(back, offset, size):
    return jnp.where(back == 1, lax.rem(size - offset, size), offset)


def shot_at(me, d, back):
    x = lax.rem(me // 16 + d // 16, 2)
    z = lax.rem(lax.rem(me // 4, 4) + turned(back, lax.rem(d // 4, 4), 4), 4)
    y = lax.rem(lax.rem(me, 4) + turned(back, lax.rem(d, 4), 4), 4)
    return x * 16 + z * 4 + y


def shot_peer_of(me, me_freq, n):
    return shot_at(me, lax.rem(n * 19, N_SHOT), lax.rem(me_freq, 2))


def shot_source_of(me, me_freq, n):
    return shot_at(me, lax.rem(n * 19, N_SHOT), 1 - lax.rem(me_freq, 2))


def any_peer_of(me, me_freq, n):
    core = lax.rem(me_freq, 2)
    d = lax.rem(n * 43, N_DEV)
    x = lax.rem((me_freq // 2) * 2 + me // 16 + turned(core, lax.rem(d // 16, 4), 4), 4)
    z = lax.rem(lax.rem(me // 4, 4) + turned(core, lax.rem(d // 4, 4), 4), 4)
    y = lax.rem(lax.rem(me, 4) + turned(core, lax.rem(d, 4), 4), 4)
    other = lax.rem(core + d // 64, 2)
    return lax.rem(x, 2) * 16 + z * 4 + y, (x // 2) * 2 + other


def fused_kernel(
    damping, gain,
    owners_ref, rec_ref, shot_ref, ct_ref, rt_ref,
    out_ref, filt_ref,
    block, wide, narrow, coeffs, xb, cb, pb, w_ref, corr, arrived, parts, answer, resp_ref, ext_ref, sb,
    load_sem, own_sem, dsend, drecv, csend, crecv, qsend, qrecv, fsend, frecv, rsend, rrecv, send_sem, recv_sem,
):
    me = lax.axis_index("shot")
    me_freq = lax.axis_index("freq")
    mine = me * N_FREQ + me_freq
    freqs = rec_ref.shape[1]
    rows = 2 * freqs
    width = R // N_FREQ

    def remote(src, dst, send, recv, device):
        return pltpu.make_async_remote_copy(
            src_ref=src, dst_ref=dst, send_sem=send, recv_sem=recv, device_id=device, device_id_type=MESH
        )

    def data_copy(n):
        peer = shot_peer_of(me, me_freq, n)
        return remote(
            rec_ref.at[:, pl.ds(peer * FL, FL)], xb.at[me], dsend.at[n], drecv.at[n], (peer, me_freq)
        )

    def coeff_copy(n):
        peer = shot_peer_of(me, me_freq, n)
        return remote(
            coeffs.at[pl.ds(peer * FL, FL)], cb.at[me], csend.at[n], crecv.at[n], (peer, me_freq)
        )

    def corr_copy(n):
        peer = shot_source_of(me, me_freq, n)
        return remote(corr.at[peer], arrived.at[me], qsend.at[n], qrecv.at[n], (peer, me_freq))

    def part_copy(e):
        other = lax.rem(me_freq + e, N_FREQ)
        return remote(parts.at[me_freq], parts.at[me_freq], fsend.at[e], frecv.at[e], (me, other))

    def resp_copy(n):
        peer = shot_peer_of(me, me_freq, n)
        return remote(answer.at[peer], resp_ref.at[me], rsend.at[n], rrecv.at[n], (peer, me_freq))

    def residual_copy(n):
        return remote(
            sb.at[n], out_ref.at[mine], send_sem.at[n], recv_sem.at[n], any_peer_of(me, me_freq, n)
        )

    def run(first, last, action):
        def step(n, carry):
            action(n)
            return carry

        lax.fori_loop(first, last, step, 0)

    def load(b):
        return pltpu.make_async_copy(
            rec_ref.at[:, :, pl.ds(b * BLK, BLK), :], block.at[b % 2], load_sem.at[b % 2]
        )

    load(0).start()
    barrier = pltpu.get_barrier_semaphore()
    run(
        1,
        N_DEV,
        lambda n: pl.semaphore_signal(
            barrier, 1, device_id=any_peer_of(me, me_freq, n), device_id_type=MESH
        ),
    )
    pl.semaphore_wait(barrier, N_DEV - 1)

    def send_next(copy, n):
        copy(n - WINDOW).wait_send()
        copy(n).start()

    for n in range(1, WINDOW + 1):
        data_copy(n).start()
    own = pltpu.make_async_copy(rec_ref.at[:, pl.ds(me * FL, FL)], xb.at[me], own_sem.at[0])
    own.start()
    slot = lax.broadcasted_iota(jnp.int32, (4 * SD, R), 0)
    key = jnp.where(slot < SD, owners_ref[0] * SD + slot, owners_ref[1] * SD + slot - SD)
    key = jnp.where(slot < 2 * SD, key, owners_ref[2] * SD + slot - 2 * SD)
    key = jnp.where(slot < 3 * SD, key, -1)
    for b in range(SD // BLK):
        if b + 1 < SD // BLK:
            load(b + 1).start()
        load(b).wait()
        for ch in range(R // 128):
            part = block[b % 2, :, :, :, ch * 128 : (ch + 1) * 128]
            wide[ch] = part.astype(jnp.float32).reshape(rows * BLK, 128)

        def bin_shot(m, carry):
            data = jnp.concatenate(
                [wide[ch, pl.ds(m, rows, stride=BLK), :] for ch in range(R // 128)], axis=1
            ).astype(jnp.bfloat16)
            where = shot_ref[pl.ds(b * BLK + m, 1), :]
            one_hot = (jnp.broadcast_to(where, key.shape) == key).astype(jnp.bfloat16)
            out = lax.dot_general(
                data, one_hot, (((1,), (1,)), ((), ())), preferred_element_type=jnp.float32
            )
            real, imag = out[:freqs], out[freqs:]
            narrow[0, pl.ds(m, freqs, stride=BLK), :] = real[:, :128]
            narrow[1, pl.ds(m, freqs, stride=BLK), :] = real[:, 128:] + pltpu.roll(imag[:, 128:], SD, 1)
            narrow[2, pl.ds(m, freqs, stride=BLK), :] = imag[:, :128]
            due = b * BLK + m

            @pl.when((lax.rem(due, 2) == 0) & (due // 2 + WINDOW + 1 < N_SHOT))
            def _():
                send_next(data_copy, due // 2 + WINDOW + 1)

            return carry

        lax.fori_loop(0, BLK, bin_shot, 0)
        for ch in range(3):
            part = narrow[ch].reshape(freqs, BLK, 128).astype(jnp.bfloat16)
            coeffs[:, b * BLK : (b + 1) * BLK, ch * 128 : (ch + 1) * 128] = part
    kept = pltpu.make_async_copy(coeffs.at[pl.ds(me * FL, FL)], cb.at[me], own_sem.at[1])
    kept.start()

    def data_to_coeff(n):
        data_copy(N_SHOT - 1 - WINDOW + n).wait_send()
        coeff_copy(n).start()

    run(1, WINDOW + 1, data_to_coeff)
    run(WINDOW + 1, N_SHOT, lambda n: send_next(coeff_copy, n))
    own.wait()
    kept.wait()
    run(1, N_SHOT, lambda n: data_copy(n).wait_recv())

    for j in range(FL):
        for t in range(STEPS):
            owner = owners_ref[t]
            real, imag = xb[owner, 0, j], xb[owner, 1, j]
            under = 3 if t == 2 else 4 + t
            top = slice(t * SD, (t + 1) * SD)
            low = slice(under * SD, (under + 1) * SD)
            w_ref[j, top, :R] = real
            w_ref[j, top, R:] = imag
            w_ref[j, low, :R] = -imag
            w_ref[j, low, R:] = real

    lane = lax.broadcasted_iota(jnp.int32, (GROUP * SD, 128), 1)

    def predict_group(g, carry):
        for i in range(GROUP):
            if i == 0:

                @pl.when(g > 0)
                def _():
                    coeff_copy(g * GROUP).wait_recv()
            else:
                coeff_copy(g * GROUP + i).wait_recv()
        shots = [shot_source_of(me, me_freq, g * GROUP + i) for i in range(GROUP)]
        cols = jnp.zeros((GROUP * SD, 128), jnp.float32)
        for j in range(FL):
            lhs = jnp.concatenate([cb[s, j] for s in shots], axis=0)
            acc = jnp.dot(lhs, w_ref[j], preferred_element_type=jnp.float32)
            pred = (gain * acc).astype(jnp.bfloat16)
            pr, pi = pred[:, :R], pred[:, R:]
            for i, s in enumerate(shots):
                pb[s, 0, j] = pr[i * SD : (i + 1) * SD]
                pb[s, 1, j] = pi[i * SD : (i + 1) * SD]
            pr, pi = pr.astype(jnp.float32), pi.astype(jnp.float32)
            xr = jnp.concatenate([xb[s, 0, j] for s in shots], axis=0).astype(jnp.float32)
            xi = jnp.concatenate([xb[s, 1, j] for s in shots], axis=0).astype(jnp.float32)
            spec = jnp.sum(pr * pr + pi * pi, axis=1, keepdims=True)
            cr = jnp.sum(pr * xr + pi * xi, axis=1, keepdims=True)
            ci = jnp.sum(pr * xi - pi * xr, axis=1, keepdims=True)
            for q, col in enumerate((spec, cr, ci)):
                cols = jnp.where(lane == 3 * j + q, col, cols)
        flat = cols.T[:8]
        for i, s in enumerate(shots):
            pair = flat[:, (i // 2) * 128 : (i // 2) * 128 + 128]
            corr[s] = pair if i % 2 == 0 else pltpu.roll(pair, SD, 1)
        for i in range(GROUP):
            if i == 0:

                @pl.when(g > 0)
                def _():
                    corr_copy(g * GROUP).start()
            else:
                corr_copy(g * GROUP + i).start()
        return carry

    lax.fori_loop(0, N_SHOT // GROUP, predict_group, 0)
    arrived[me] = corr[me]
    run(1, N_SHOT, lambda n: corr_copy(n).wait_recv())

    parts[me_freq] = jnp.dot(
        ct_ref[...],
        arrived[...].reshape(N_SHOT * 8, 128),
        precision=HIGH,
        preferred_element_type=jnp.float32,
    )
    for e in range(1, N_FREQ):
        part_copy(e).start()
    for e in range(1, N_FREQ):
        part_copy(e).wait()
    total = parts[0]
    for e in range(1, N_FREQ):
        total = total + parts[e]
    row64 = lax.broadcasted_iota(jnp.int32, (64, 128), 0)
    row = lax.broadcasted_iota(jnp.int32, (32, 128), 0)
    ext_ref[...] = total[:64] + jnp.where(row64 == TAPS - 1, damping, 0.0)
    rhs = total[64:] + jnp.where(row == HALF, damping, 0.0)
    cols = [ext_ref[pl.ds(TAPS - 1 - k, 32), :] for k in range(TAPS)]
    inverse = []
    for p in range(TAPS):
        inv = 1.0 / cols[p][p : p + 1, :]
        inverse.append(inv)
        if p == TAPS - 1:
            break
        factor = jnp.where(row > p, cols[p] * inv, 0.0)
        rhs = rhs - factor * rhs[p : p + 1, :]
        for k in range(p + 1, TAPS):
            cols[k] = cols[k] - factor * cols[k][p : p + 1, :]
    found = jnp.zeros((32, 128), jnp.float32)
    for p in range(TAPS - 1, -1, -1):
        value = rhs[p : p + 1, :] * inverse[p]
        found = jnp.where(row == p, value, found)
        rhs = rhs - cols[p] * value
    resp = jnp.dot(rt_ref[...], found, precision=HIGH, preferred_element_type=jnp.float32)
    answer[...] = resp.reshape(N_SHOT, 8, 128)
    run(1, N_SHOT, lambda n: resp_copy(n).start())
    resp_ref[me] = answer[me]
    filt_ref[...] = jnp.concatenate([found, jnp.zeros((96, 128), jnp.float32)], axis=0).T[:SD]
    run(1, N_SHOT, lambda n: resp_copy(n).wait_recv())

    diagonal = lax.broadcasted_iota(jnp.int32, (SD, 128), 0) == lax.broadcasted_iota(
        jnp.int32, (SD, 128), 1
    )

    def compute(n):
        shot, freq = any_peer_of(me, me_freq, n)
        resp = resp_ref[shot]
        part = pl.ds(pl.multiple_of(freq * width, width), width)

        def column(q):
            spread = jnp.broadcast_to(resp[q : q + 1], (SD, 128))
            return jnp.sum(jnp.where(diagonal, spread, 0.0), axis=1, keepdims=True)

        for j in range(FL):
            real, imag = column(j), column(FL + j)
            xr = xb[shot, 0, j, :, part].astype(jnp.float32)
            xi = xb[shot, 1, j, :, part].astype(jnp.float32)
            pr = pb[shot, 0, j, :, part].astype(jnp.float32)
            pi = pb[shot, 1, j, :, part].astype(jnp.float32)
            sb[n, 0, j] = (xr - (real * pr - imag * pi)).astype(jnp.bfloat16)
            sb[n, 1, j] = (xi - (real * pi + imag * pr)).astype(jnp.bfloat16)

    def residual_step(n):
        compute(n)
        residual_copy(n).start()

    run(1, N_DEV, residual_step)
    compute(0)
    stay = pltpu.make_async_copy(sb.at[0], out_ref.at[mine], own_sem.at[2])
    stay.start()
    stay.wait()
    run(N_SHOT - WINDOW, N_SHOT, lambda n: coeff_copy(n).wait_send())
    run(1, N_SHOT, lambda n: corr_copy(n).wait_send())
    run(1, N_SHOT, lambda n: resp_copy(n).wait_send())
    run(1, N_DEV, lambda n: residual_copy(n).wait())


def fused(owners, recorded, rec_shot, ct, rt, damping, gain):
    freqs = recorded.shape[1]
    width = 2 * STEPS * SD
    anywhere = pl.BlockSpec(memory_space=pl.ANY)
    whole = pl.BlockSpec(memory_space=pltpu.VMEM)
    slab = (N_SHOT, 2, FL, SD, R)
    small = (N_SHOT, 8, 128)
    pairs = [N_SHOT, N_SHOT, N_SHOT, N_FREQ, N_SHOT, N_DEV]
    return pl.pallas_call(
        lambda *refs: fused_kernel(damping, gain, *refs),
        in_specs=[pl.BlockSpec(memory_space=pltpu.SMEM), anywhere, whole, whole, whole],
        out_specs=[anywhere, whole],
        out_shape=(
            jax.ShapeDtypeStruct((N_DEV, 2, FL, SD, R // N_FREQ), jnp.bfloat16),
            jax.ShapeDtypeStruct((SD, 128), jnp.float32),
        ),
        scratch_shapes=[
            pltpu.VMEM((2, 2, freqs, BLK, R), jnp.bfloat16),
            pltpu.VMEM((R // 128, 2 * freqs * BLK, 128), jnp.float32),
            pltpu.VMEM((3, freqs * BLK, 128), jnp.float32),
            pltpu.VMEM((freqs, SD, width), jnp.bfloat16),
            pltpu.VMEM(slab, jnp.bfloat16),
            pltpu.VMEM((N_SHOT, FL, SD, width), jnp.bfloat16),
            pltpu.VMEM(slab, jnp.bfloat16),
            pltpu.VMEM((FL, width, 2 * R), jnp.bfloat16),
            pltpu.VMEM(small, jnp.float32),
            pltpu.VMEM(small, jnp.float32),
            pltpu.VMEM((N_FREQ, 96, 128), jnp.float32),
            pltpu.VMEM(small, jnp.float32),
            pltpu.VMEM(small, jnp.float32),
            pltpu.VMEM((64, 128), jnp.float32),
            pltpu.VMEM((N_DEV, 2, FL, SD, R // N_FREQ), jnp.bfloat16),
            pltpu.SemaphoreType.DMA((2,)),
            pltpu.SemaphoreType.DMA((3,)),
        ]
        + [pltpu.SemaphoreType.DMA((count,)) for count in pairs for _ in range(2)],
        compiler_params=pltpu.CompilerParams(
            collective_id=0, has_side_effects=True, vmem_limit_bytes=LIMIT
        ),
        name="fused",
    )(owners, recorded, rec_shot, ct, rt)


def transform_kernel(r_ref, t_ref, *rest):
    out_ref, wide_ref = rest[-2:]
    k = r_ref.shape[0]
    s = r_ref.shape[1]
    wide_ref[...] = r_ref[...].astype(jnp.float32).reshape(k * s, 128)
    group = 4
    for m in range(0, s, group):
        rows = jnp.concatenate(
            [wide_ref[pl.ds(m + g, k, stride=s), :].T.astype(jnp.bfloat16) for g in range(group)], axis=0
        )
        out = jnp.dot(rows, t_ref[...], preferred_element_type=jnp.float32).astype(jnp.bfloat16)
        out_ref[m : m + group] = out.reshape(group, 128, 2 * F)


def transform(spectra, table, chunk, before):
    k, shots, recv = spectra.shape
    step = 16
    base = chunk * (shots // step)
    in_specs = [
        pl.BlockSpec((k, step, recv), lambda i: (0, i, 0)),
        pl.BlockSpec((k, 2 * F), lambda i: (0, 0)),
    ]
    args = [spectra, table]
    alias = {}
    if before is not None:
        in_specs.append(pl.BlockSpec(memory_space=pl.ANY))
        args.append(before)
        alias = {2: 0}
    return pl.pallas_call(
        transform_kernel,
        grid=(shots // step,),
        in_specs=in_specs,
        out_specs=pl.BlockSpec((step, recv, 2 * F), lambda i: (i + base, 0, 0)),
        out_shape=jax.ShapeDtypeStruct((SD, recv, 2 * F), jnp.bfloat16),
        scratch_shapes=[pltpu.VMEM((k * step, recv), jnp.float32)],
        input_output_aliases=alias,
        compiler_params=pltpu.CompilerParams(
            dimension_semantics=("arbitrary",), vmem_limit_bytes=LIMIT
        ),
        cost_estimate=pl.CostEstimate(flops=2 * 10**9, bytes_accessed=12 * 10**6, transcendentals=0),
        name=f"transform{chunk}",
    )(*args)


def per_device(recorded, rec_shot, owners):
    gain = (N_SHOT / (2.0 * R * STEPS)) ** 0.5
    me_freq = lax.axis_index("freq")
    ct = lax.dynamic_index_in_dim(jnp.asarray(corr_table()), me_freq, 0, False)
    rt = lax.dynamic_index_in_dim(jnp.asarray(resp_table()), me_freq, 0, False)
    table = jnp.asarray(time_table(), dtype=jnp.bfloat16)
    res, filt = fused(owners, recorded, rec_shot, ct, rt, REG * R * F, gain)
    primaries = transform(res.reshape(2 * F, SD, R // N_FREQ), table, 0, None)
    return (primaries, filt[:, :TAPS])


def solution(mesh):
    placed = (P(None, "freq", "shot", None), P("shot", None), P())
    return jax.shard_map(
        per_device,
        mesh=mesh,
        in_specs=placed,
        out_specs=(P("shot", "freq", None), P("shot", None)),
        check_vma=False,
    )
```

```python
import math

import jax
import jax.numpy as jnp
import numpy as np
from jax import lax
from jax.experimental import pallas as pl
from jax.experimental.pallas import tpu as pltpu
from jax.sharding import PartitionSpec as P

F = 256
TAPS = 31
STEPS = 3
HALF = (TAPS - 1) // 2
REG = 2.0
N_SHOT = 32
N_FREQ = 4
N_DEV = N_SHOT * N_FREQ
FL = F // N_DEV
SD = 64
R = 512
BLK = 16
MIB = 1 << 20
LIMIT = 60 * MIB
GROUP = 4
AHEAD = 16
WINDOW = 8
HIGH = lax.Precision.HIGHEST
MESH = pl.DeviceIdType.MESH


def device_freqs():
    dev = np.arange(N_DEV)
    return (dev % N_FREQ)[:, None] * (F // N_FREQ) + (dev // N_FREQ)[:, None] * FL + np.arange(FL)[None, :]


def angle(freq, step):
    return ((freq * step) % (2 * F)).astype(np.float64) * (2.0 * math.pi / (2 * F))


def corr_table():
    freqs = device_freqs().reshape(N_SHOT, N_FREQ, FL)
    lags = np.abs(np.arange(64) - (TAPS - 1))
    taps = np.arange(32) - HALF
    table = np.zeros((N_FREQ, 96, N_SHOT, 8))
    for j in range(FL):
        col = freqs[:, :, j].T[:, None, :]
        table[:, :64, :, 3 * j] = np.cos(angle(col, lags[None, :, None]))
        table[:, 64:, :, 3 * j + 1] = np.cos(angle(col, taps[None, :, None]))
        table[:, 64:, :, 3 * j + 2] = -np.sin(angle(col, taps[None, :, None]))
    return table.reshape(N_FREQ, 96, N_SHOT * 8).astype(np.float32)


def resp_table():
    freqs = device_freqs().reshape(N_SHOT, N_FREQ, FL)
    taps = np.arange(32) - HALF
    valid = np.arange(32) < TAPS
    table = np.zeros((N_FREQ, N_SHOT, 8, 32))
    for j in range(FL):
        ang = angle(freqs[:, :, j].T[:, :, None], taps[None, None, :])
        table[:, :, j] = np.cos(ang) * valid
        table[:, :, FL + j] = -np.sin(ang) * valid
    return table.reshape(N_FREQ, N_SHOT * 8, 32).astype(np.float32)


def time_table():
    freqs = device_freqs()
    ang = angle(freqs[:, :, None], np.arange(2 * F)[None, None, :])
    norm = 1.0 / math.sqrt(F)
    table = np.stack([np.cos(ang) * norm, -np.sin(ang) * norm], axis=1)
    return table.reshape(2 * F, 2 * F).astype(np.float32)


def turned(back, offset, size):
    return jnp.where(back == 1, lax.rem(size - offset, size), offset)


def shot_at(me, d, back):
    x = lax.rem(me // 16 + d // 16, 2)
    z = lax.rem(lax.rem(me // 4, 4) + turned(back, lax.rem(d // 4, 4), 4), 4)
    y = lax.rem(lax.rem(me, 4) + turned(back, lax.rem(d, 4), 4), 4)
    return x * 16 + z * 4 + y


def shot_peer_of(me, me_freq, n):
    return shot_at(me, lax.rem(n * 19, N_SHOT), lax.rem(me_freq, 2))


def shot_source_of(me, me_freq, n):
    return shot_at(me, lax.rem(n * 19, N_SHOT), 1 - lax.rem(me_freq, 2))


def any_peer_of(me, me_freq, n):
    core = lax.rem(me_freq, 2)
    d = lax.rem(n * 43, N_DEV)
    x = lax.rem((me_freq // 2) * 2 + me // 16 + turned(core, lax.rem(d // 16, 4), 4), 4)
    z = lax.rem(lax.rem(me // 4, 4) + turned(core, lax.rem(d // 4, 4), 4), 4)
    y = lax.rem(lax.rem(me, 4) + turned(core, lax.rem(d, 4), 4), 4)
    other = lax.rem(core + d // 64, 2)
    return lax.rem(x, 2) * 16 + z * 4 + y, (x // 2) * 2 + other


def fused_kernel(
    damping, gain,
    owners_ref, rec_ref, shot_ref, cts_ref, rts_ref,
    out_ref, filt_ref,
    block, wide, narrow, coeffs, xb, cb, pb, w_ref, corr, arrived, parts, answer, resp_ref, ext_ref, sb, ct_ref, rt_ref,
    load_sem, own_sem, dsend, drecv, csend, crecv, qsend, qrecv, fsend, frecv, rsend, rrecv, send_sem, recv_sem,
):
    me = lax.axis_index("shot")
    me_freq = lax.axis_index("freq")
    mine = me * N_FREQ + me_freq
    freqs = rec_ref.shape[1]
    rows = 2 * freqs
    width = R // N_FREQ

    def remote(src, dst, send, recv, device):
        return pltpu.make_async_remote_copy(
            src_ref=src, dst_ref=dst, send_sem=send, recv_sem=recv, device_id=device, device_id_type=MESH
        )

    def data_copy(n):
        peer = shot_peer_of(me, me_freq, n)
        return remote(
            rec_ref.at[:, pl.ds(peer * FL, FL)], xb.at[me], dsend.at[n], drecv.at[n], (peer, me_freq)
        )

    def coeff_copy(n):
        peer = shot_peer_of(me, me_freq, n)
        return remote(
            coeffs.at[pl.ds(peer * FL, FL)], cb.at[me], csend.at[n], crecv.at[n], (peer, me_freq)
        )

    def corr_copy(n):
        peer = shot_source_of(me, me_freq, n)
        return remote(corr.at[peer], arrived.at[me], qsend.at[n], qrecv.at[n], (peer, me_freq))

    def part_copy(e):
        other = lax.rem(me_freq + e, N_FREQ)
        return remote(parts.at[me_freq], parts.at[me_freq], fsend.at[e], frecv.at[e], (me, other))

    def resp_copy(n):
        peer = shot_peer_of(me, me_freq, n)
        return remote(answer.at[peer], resp_ref.at[me], rsend.at[n], rrecv.at[n], (peer, me_freq))

    def residual_copy(n):
        return remote(
            sb.at[n], out_ref.at[mine], send_sem.at[n], recv_sem.at[n], any_peer_of(me, me_freq, n)
        )

    def run(first, last, action):
        def step(n, carry):
            action(n)
            return carry

        lax.fori_loop(first, last, step, 0)

    def load(b):
        return pltpu.make_async_copy(
            rec_ref.at[:, :, pl.ds(b * BLK, BLK), :], block.at[b % 2], load_sem.at[b % 2]
        )

    tables = (
        pltpu.make_async_copy(cts_ref.at[me_freq], ct_ref, own_sem.at[3]),
        pltpu.make_async_copy(rts_ref.at[me_freq], rt_ref, own_sem.at[4]),
    )

    load(0).start()
    for table in tables:
        table.start()
    barrier = pltpu.get_barrier_semaphore()
    run(
        1,
        N_SHOT,
        lambda n: pl.semaphore_signal(
            barrier, 1, device_id=(shot_peer_of(me, me_freq, n), me_freq), device_id_type=MESH
        ),
    )
    for e in range(1, N_FREQ):
        pl.semaphore_signal(
            barrier, 1, device_id=(me, lax.rem(me_freq + e, N_FREQ)), device_id_type=MESH
        )
    pl.semaphore_wait(barrier, N_SHOT + N_FREQ - 2)

    def send_next(copy, n):
        copy(n - WINDOW).wait_send()
        copy(n).start()

    for n in range(1, WINDOW + 1):
        data_copy(n).start()
    own = pltpu.make_async_copy(rec_ref.at[:, pl.ds(me * FL, FL)], xb.at[me], own_sem.at[0])
    own.start()
    slot = lax.broadcasted_iota(jnp.int32, (4 * SD, R), 0)
    key = jnp.where(slot < SD, owners_ref[0] * SD + slot, owners_ref[1] * SD + slot - SD)
    key = jnp.where(slot < 2 * SD, key, owners_ref[2] * SD + slot - 2 * SD)
    key = jnp.where(slot < 3 * SD, key, -1)
    for b in range(SD // BLK):
        if b + 1 < SD // BLK:
            load(b + 1).start()
        load(b).wait()
        for ch in range(R // 128):
            part = block[b % 2, :, :, :, ch * 128 : (ch + 1) * 128]
            wide[ch] = part.astype(jnp.float32).reshape(rows * BLK, 128)

        def bin_shot(m, carry):
            data = jnp.concatenate(
                [wide[ch, pl.ds(m, rows, stride=BLK), :] for ch in range(R // 128)], axis=1
            ).astype(jnp.bfloat16)
            where = shot_ref[pl.ds(b * BLK + m, 1), :]
            one_hot = (jnp.broadcast_to(where, key.shape) == key).astype(jnp.bfloat16)
            out = lax.dot_general(
                data, one_hot, (((1,), (1,)), ((), ())), preferred_element_type=jnp.float32
            )
            real, imag = out[:freqs], out[freqs:]
            narrow[0, pl.ds(m, freqs, stride=BLK), :] = real[:, :128]
            narrow[1, pl.ds(m, freqs, stride=BLK), :] = real[:, 128:] + pltpu.roll(imag[:, 128:], SD, 1)
            narrow[2, pl.ds(m, freqs, stride=BLK), :] = imag[:, :128]
            due = b * BLK + m

            @pl.when((lax.rem(due, 2) == 0) & (due // 2 + WINDOW + 1 < N_SHOT))
            def _():
                send_next(data_copy, due // 2 + WINDOW + 1)

            return carry

        lax.fori_loop(0, BLK, bin_shot, 0)
        for ch in range(3):
            part = narrow[ch].reshape(freqs, BLK, 128).astype(jnp.bfloat16)
            coeffs[:, b * BLK : (b + 1) * BLK, ch * 128 : (ch + 1) * 128] = part
    kept = pltpu.make_async_copy(coeffs.at[pl.ds(me * FL, FL)], cb.at[me], own_sem.at[1])
    kept.start()

    def data_to_coeff(n):
        data_copy(N_SHOT - 1 - WINDOW + n).wait_send()
        coeff_copy(n).start()

    run(1, WINDOW + 1, data_to_coeff)
    run(WINDOW + 1, AHEAD, lambda n: coeff_copy(n).start())
    own.wait()
    kept.wait()
    run(1, N_SHOT, lambda n: data_copy(n).wait_recv())

    for j in range(FL):
        for t in range(STEPS):
            owner = owners_ref[t]
            real, imag = xb[owner, 0, j], xb[owner, 1, j]
            under = 3 if t == 2 else 4 + t
            top = slice(t * SD, (t + 1) * SD)
            low = slice(under * SD, (under + 1) * SD)
            w_ref[j, top, :R] = real
            w_ref[j, top, R:] = imag
            w_ref[j, low, :R] = -imag
            w_ref[j, low, R:] = real

    lane = lax.broadcasted_iota(jnp.int32, (GROUP * SD, 128), 1)

    def predict_group(g, carry):
        for i in range(GROUP):
            if i == 0:

                @pl.when(g > 0)
                def _():
                    coeff_copy(g * GROUP).wait_recv()
            else:
                coeff_copy(g * GROUP + i).wait_recv()

        @pl.when(AHEAD + g * GROUP < N_SHOT)
        def _():
            for i in range(GROUP):
                coeff_copy(AHEAD + g * GROUP + i).start()

        shots = [shot_source_of(me, me_freq, g * GROUP + i) for i in range(GROUP)]
        cols = jnp.zeros((GROUP * SD, 128), jnp.float32)
        for j in range(FL):
            lhs = jnp.concatenate([cb[s, j] for s in shots], axis=0)
            acc = jnp.dot(lhs, w_ref[j], preferred_element_type=jnp.float32)
            pred = (gain * acc).astype(jnp.bfloat16)
            pr, pi = pred[:, :R], pred[:, R:]
            for i, s in enumerate(shots):
                pb[s, 0, j] = pr[i * SD : (i + 1) * SD]
                pb[s, 1, j] = pi[i * SD : (i + 1) * SD]
            pr, pi = pr.astype(jnp.float32), pi.astype(jnp.float32)
            xr = jnp.concatenate([xb[s, 0, j] for s in shots], axis=0).astype(jnp.float32)
            xi = jnp.concatenate([xb[s, 1, j] for s in shots], axis=0).astype(jnp.float32)
            spec = jnp.sum(pr * pr + pi * pi, axis=1, keepdims=True)
            cr = jnp.sum(pr * xr + pi * xi, axis=1, keepdims=True)
            ci = jnp.sum(pr * xi - pi * xr, axis=1, keepdims=True)
            for q, col in enumerate((spec, cr, ci)):
                cols = jnp.where(lane == 3 * j + q, col, cols)
        flat = cols.T[:8]
        for i, s in enumerate(shots):
            pair = flat[:, (i // 2) * 128 : (i // 2) * 128 + 128]
            corr[s] = pair if i % 2 == 0 else pltpu.roll(pair, SD, 1)
        for i in range(GROUP):
            if i == 0:

                @pl.when(g > 0)
                def _():
                    corr_copy(g * GROUP).start()
            else:
                corr_copy(g * GROUP + i).start()
        return carry

    lax.fori_loop(0, N_SHOT // GROUP, predict_group, 0)
    arrived[me] = corr[me]
    run(1, N_SHOT, lambda n: corr_copy(n).wait_recv())

    for table in tables:
        table.wait()
    parts[me_freq] = jnp.dot(
        ct_ref[...],
        arrived[...].reshape(N_SHOT * 8, 128),
        precision=HIGH,
        preferred_element_type=jnp.float32,
    )
    for e in range(1, N_FREQ):
        part_copy(e).start()
    for e in range(1, N_FREQ):
        part_copy(e).wait()
    total = parts[0]
    for e in range(1, N_FREQ):
        total = total + parts[e]
    row64 = lax.broadcasted_iota(jnp.int32, (64, 128), 0)
    row = lax.broadcasted_iota(jnp.int32, (32, 128), 0)
    ext_ref[...] = total[:64] + jnp.where(row64 == TAPS - 1, damping, 0.0)
    rhs = total[64:] + jnp.where(row == HALF, damping, 0.0)
    cols = [ext_ref[pl.ds(TAPS - 1 - k, 32), :] for k in range(TAPS)]
    inverse = []
    for p in range(TAPS):
        inv = 1.0 / cols[p][p : p + 1, :]
        inverse.append(inv)
        if p == TAPS - 1:
            break
        factor = jnp.where(row > p, cols[p] * inv, 0.0)
        rhs = rhs - factor * rhs[p : p + 1, :]
        for k in range(p + 1, TAPS):
            cols[k] = cols[k] - factor * cols[k][p : p + 1, :]
    found = jnp.zeros((32, 128), jnp.float32)
    for p in range(TAPS - 1, -1, -1):
        value = rhs[p : p + 1, :] * inverse[p]
        found = jnp.where(row == p, value, found)
        rhs = rhs - cols[p] * value
    resp = jnp.dot(rt_ref[...], found, precision=HIGH, preferred_element_type=jnp.float32)
    answer[...] = resp.reshape(N_SHOT, 8, 128)
    run(1, N_SHOT, lambda n: resp_copy(n).start())
    resp_ref[me] = answer[me]
    filt_ref[...] = jnp.concatenate([found, jnp.zeros((96, 128), jnp.float32)], axis=0).T[:SD]
    run(1, N_SHOT, lambda n: resp_copy(n).wait_recv())

    diagonal = lax.broadcasted_iota(jnp.int32, (SD, 128), 0) == lax.broadcasted_iota(
        jnp.int32, (SD, 128), 1
    )

    def compute(n):
        shot, freq = any_peer_of(me, me_freq, n)
        resp = resp_ref[shot]
        part = pl.ds(pl.multiple_of(freq * width, width), width)

        def column(q):
            spread = jnp.broadcast_to(resp[q : q + 1], (SD, 128))
            return jnp.sum(jnp.where(diagonal, spread, 0.0), axis=1, keepdims=True)

        for j in range(FL):
            real, imag = column(j), column(FL + j)
            xr = xb[shot, 0, j, :, part].astype(jnp.float32)
            xi = xb[shot, 1, j, :, part].astype(jnp.float32)
            pr = pb[shot, 0, j, :, part].astype(jnp.float32)
            pi = pb[shot, 1, j, :, part].astype(jnp.float32)
            sb[n, 0, j] = (xr - (real * pr - imag * pi)).astype(jnp.bfloat16)
            sb[n, 1, j] = (xi - (real * pi + imag * pr)).astype(jnp.bfloat16)

    def residual_step(n):
        compute(n)
        residual_copy(n).start()

    run(1, N_DEV, residual_step)
    compute(0)
    stay = pltpu.make_async_copy(sb.at[0], out_ref.at[mine], own_sem.at[2])
    stay.start()
    stay.wait()
    run(1, N_SHOT, lambda n: coeff_copy(n).wait_send())
    run(1, N_SHOT, lambda n: corr_copy(n).wait_send())
    run(1, N_SHOT, lambda n: resp_copy(n).wait_send())
    run(1, N_DEV, lambda n: residual_copy(n).wait())


def fused(owners, recorded, rec_shot, ct, rt, damping, gain):
    freqs = recorded.shape[1]
    width = 2 * STEPS * SD
    anywhere = pl.BlockSpec(memory_space=pl.ANY)
    whole = pl.BlockSpec(memory_space=pltpu.VMEM)
    slab = (N_SHOT, 2, FL, SD, R)
    small = (N_SHOT, 8, 128)
    pairs = [N_SHOT, N_SHOT, N_SHOT, N_FREQ, N_SHOT, N_DEV]
    return pl.pallas_call(
        lambda *refs: fused_kernel(damping, gain, *refs),
        in_specs=[pl.BlockSpec(memory_space=pltpu.SMEM), anywhere, whole, anywhere, anywhere],
        out_specs=[anywhere, whole],
        out_shape=(
            jax.ShapeDtypeStruct((N_DEV, 2, FL, SD, R // N_FREQ), jnp.bfloat16),
            jax.ShapeDtypeStruct((SD, 128), jnp.float32),
        ),
        scratch_shapes=[
            pltpu.VMEM((2, 2, freqs, BLK, R), jnp.bfloat16),
            pltpu.VMEM((R // 128, 2 * freqs * BLK, 128), jnp.float32),
            pltpu.VMEM((3, freqs * BLK, 128), jnp.float32),
            pltpu.VMEM((freqs, SD, width), jnp.bfloat16),
            pltpu.VMEM(slab, jnp.bfloat16),
            pltpu.VMEM((N_SHOT, FL, SD, width), jnp.bfloat16),
            pltpu.VMEM(slab, jnp.bfloat16),
            pltpu.VMEM((FL, width, 2 * R), jnp.bfloat16),
            pltpu.VMEM(small, jnp.float32),
            pltpu.VMEM(small, jnp.float32),
            pltpu.VMEM((N_FREQ, 96, 128), jnp.float32),
            pltpu.VMEM(small, jnp.float32),
            pltpu.VMEM(small, jnp.float32),
            pltpu.VMEM((64, 128), jnp.float32),
            pltpu.VMEM((N_DEV, 2, FL, SD, R // N_FREQ), jnp.bfloat16),
            pltpu.VMEM(ct.shape[1:], jnp.float32),
            pltpu.VMEM(rt.shape[1:], jnp.float32),
            pltpu.SemaphoreType.DMA((2,)),
            pltpu.SemaphoreType.DMA((5,)),
        ]
        + [pltpu.SemaphoreType.DMA((count,)) for count in pairs for _ in range(2)],
        compiler_params=pltpu.CompilerParams(
            collective_id=0, has_side_effects=True, vmem_limit_bytes=LIMIT
        ),
        name="fused",
    )(owners, recorded, rec_shot, ct, rt)


def transform_kernel(r_ref, t_ref, *rest):
    out_ref, wide_ref = rest[-2:]
    k = r_ref.shape[0]
    s = r_ref.shape[1]
    wide_ref[...] = r_ref[...].astype(jnp.float32).reshape(k * s, 128)
    group = 4
    for m in range(0, s, group):
        rows = jnp.concatenate(
            [wide_ref[pl.ds(m + g, k, stride=s), :].T.astype(jnp.bfloat16) for g in range(group)], axis=0
        )
        out = jnp.dot(rows, t_ref[...], preferred_element_type=jnp.float32).astype(jnp.bfloat16)
        out_ref[m : m + group] = out.reshape(group, 128, 2 * F)


def transform(spectra, table, chunk, before):
    k, shots, recv = spectra.shape
    step = 16
    base = chunk * (shots // step)
    in_specs = [
        pl.BlockSpec((k, step, recv), lambda i: (0, i, 0)),
        pl.BlockSpec((k, 2 * F), lambda i: (0, 0)),
    ]
    args = [spectra, table]
    alias = {}
    if before is not None:
        in_specs.append(pl.BlockSpec(memory_space=pl.ANY))
        args.append(before)
        alias = {2: 0}
    return pl.pallas_call(
        transform_kernel,
        grid=(shots // step,),
        in_specs=in_specs,
        out_specs=pl.BlockSpec((step, recv, 2 * F), lambda i: (i + base, 0, 0)),
        out_shape=jax.ShapeDtypeStruct((SD, recv, 2 * F), jnp.bfloat16),
        scratch_shapes=[pltpu.VMEM((k * step, recv), jnp.float32)],
        input_output_aliases=alias,
        compiler_params=pltpu.CompilerParams(
            dimension_semantics=("arbitrary",), vmem_limit_bytes=LIMIT
        ),
        cost_estimate=pl.CostEstimate(flops=2 * 10**9, bytes_accessed=12 * 10**6, transcendentals=0),
        name=f"transform{chunk}",
    )(*args)


def per_device(recorded, rec_shot, owners):
    gain = (N_SHOT / (2.0 * R * STEPS)) ** 0.5
    ct, rt = jnp.asarray(corr_table()), jnp.asarray(resp_table())
    table = jnp.asarray(time_table(), dtype=jnp.bfloat16)
    res, filt = fused(owners, recorded, rec_shot, ct, rt, REG * R * F, gain)
    primaries = transform(res.reshape(2 * F, SD, R // N_FREQ), table, 0, None)
    return (primaries, filt[:, :TAPS])


def solution(mesh):
    placed = (P(None, "freq", "shot", None), P("shot", None), P())
    return jax.shard_map(
        per_device,
        mesh=mesh,
        in_specs=placed,
        out_specs=(P("shot", "freq", None), P("shot", None)),
        check_vma=False,
    )
```

```python
import math

import jax
import jax.numpy as jnp
import numpy as np
from jax import lax
from jax.experimental import pallas as pl
from jax.experimental.pallas import tpu as pltpu
from jax.sharding import PartitionSpec as P

F = 256
TAPS = 31
STEPS = 3
HALF = (TAPS - 1) // 2
REG = 2.0
N_SHOT = 32
N_FREQ = 4
N_DEV = N_SHOT * N_FREQ
FL = F // N_DEV
SD = 64
R = 512
BLK = 16
MIB = 1 << 20
LIMIT = 60 * MIB
GROUP = 4
AHEAD = 16
WINDOW = 12
HIGH = lax.Precision.HIGHEST
MESH = pl.DeviceIdType.MESH


def device_freqs():
    dev = np.arange(N_DEV)
    return (dev % N_FREQ)[:, None] * (F // N_FREQ) + (dev // N_FREQ)[:, None] * FL + np.arange(FL)[None, :]


def angle(freq, step):
    return ((freq * step) % (2 * F)).astype(np.float64) * (2.0 * math.pi / (2 * F))


def corr_table():
    freqs = device_freqs().reshape(N_SHOT, N_FREQ, FL)
    lags = np.abs(np.arange(64) - (TAPS - 1))
    taps = np.arange(32) - HALF
    table = np.zeros((N_FREQ, 96, N_SHOT, 8))
    for j in range(FL):
        col = freqs[:, :, j].T[:, None, :]
        table[:, :64, :, 3 * j] = np.cos(angle(col, lags[None, :, None]))
        table[:, 64:, :, 3 * j + 1] = np.cos(angle(col, taps[None, :, None]))
        table[:, 64:, :, 3 * j + 2] = -np.sin(angle(col, taps[None, :, None]))
    return table.reshape(N_FREQ, 96, N_SHOT * 8).astype(np.float32)


def resp_table():
    freqs = device_freqs().reshape(N_SHOT, N_FREQ, FL)
    taps = np.arange(32) - HALF
    valid = np.arange(32) < TAPS
    table = np.zeros((N_FREQ, N_SHOT, 8, 32))
    for j in range(FL):
        ang = angle(freqs[:, :, j].T[:, :, None], taps[None, None, :])
        table[:, :, j] = np.cos(ang) * valid
        table[:, :, FL + j] = -np.sin(ang) * valid
    return table.reshape(N_FREQ, N_SHOT * 8, 32).astype(np.float32)


def time_table():
    freqs = device_freqs()
    ang = angle(freqs[:, :, None], np.arange(2 * F)[None, None, :])
    norm = 1.0 / math.sqrt(F)
    table = np.stack([np.cos(ang) * norm, -np.sin(ang) * norm], axis=1)
    return table.reshape(2 * F, 2 * F).astype(np.float32)


def turned(back, offset, size):
    return jnp.where(back == 1, lax.rem(size - offset, size), offset)


def shot_at(me, d, back):
    x = lax.rem(me // 16 + d // 16, 2)
    z = lax.rem(lax.rem(me // 4, 4) + turned(back, lax.rem(d // 4, 4), 4), 4)
    y = lax.rem(lax.rem(me, 4) + turned(back, lax.rem(d, 4), 4), 4)
    return x * 16 + z * 4 + y


def shot_peer_of(me, me_freq, n):
    return shot_at(me, lax.rem(n * 11, N_SHOT), lax.rem(me_freq, 2))


def shot_source_of(me, me_freq, n):
    return shot_at(me, lax.rem(n * 11, N_SHOT), 1 - lax.rem(me_freq, 2))


def any_peer_of(me, me_freq, n):
    core = lax.rem(me_freq, 2)
    d = lax.rem(n * 43, N_DEV)
    x = lax.rem((me_freq // 2) * 2 + me // 16 + turned(core, lax.rem(d // 16, 4), 4), 4)
    z = lax.rem(lax.rem(me // 4, 4) + turned(core, lax.rem(d // 4, 4), 4), 4)
    y = lax.rem(lax.rem(me, 4) + turned(core, lax.rem(d, 4), 4), 4)
    other = lax.rem(core + d // 64, 2)
    return lax.rem(x, 2) * 16 + z * 4 + y, (x // 2) * 2 + other


def fused_kernel(
    damping, gain,
    owners_ref, rec_ref, shot_ref, cts_ref, rts_ref,
    out_ref, filt_ref,
    block, wide, narrow, coeffs, xb, cb, pb, w_ref, corr, arrived, parts, answer, resp_ref, ext_ref, sb, ct_ref, rt_ref,
    load_sem, own_sem, dsend, drecv, csend, crecv, qsend, qrecv, fsend, frecv, rsend, rrecv, send_sem, recv_sem,
):
    me = lax.axis_index("shot")
    me_freq = lax.axis_index("freq")
    mine = me * N_FREQ + me_freq
    freqs = rec_ref.shape[1]
    rows = 2 * freqs
    width = R // N_FREQ

    def remote(src, dst, send, recv, device):
        return pltpu.make_async_remote_copy(
            src_ref=src, dst_ref=dst, send_sem=send, recv_sem=recv, device_id=device, device_id_type=MESH
        )

    def data_copy(n):
        peer = shot_peer_of(me, me_freq, n)
        return remote(
            rec_ref.at[:, pl.ds(peer * FL, FL)], xb.at[me], dsend.at[n], drecv.at[n], (peer, me_freq)
        )

    def coeff_copy(n):
        peer = shot_peer_of(me, me_freq, n)
        return remote(
            coeffs.at[pl.ds(peer * FL, FL)], cb.at[me], csend.at[n], crecv.at[n], (peer, me_freq)
        )

    def corr_copy(n):
        peer = shot_source_of(me, me_freq, n)
        return remote(corr.at[peer], arrived.at[me], qsend.at[n], qrecv.at[n], (peer, me_freq))

    def part_copy(e):
        other = lax.rem(me_freq + e, N_FREQ)
        return remote(parts.at[me_freq], parts.at[me_freq], fsend.at[e], frecv.at[e], (me, other))

    def resp_copy(n):
        peer = shot_peer_of(me, me_freq, n)
        return remote(answer.at[peer], resp_ref.at[me], rsend.at[n], rrecv.at[n], (peer, me_freq))

    def residual_copy(n):
        return remote(
            sb.at[n], out_ref.at[mine], send_sem.at[n], recv_sem.at[n], any_peer_of(me, me_freq, n)
        )

    def run(first, last, action):
        def step(n, carry):
            action(n)
            return carry

        lax.fori_loop(first, last, step, 0)

    def load(b):
        return pltpu.make_async_copy(
            rec_ref.at[:, :, pl.ds(b * BLK, BLK), :], block.at[b % 2], load_sem.at[b % 2]
        )

    tables = (
        pltpu.make_async_copy(cts_ref.at[me_freq], ct_ref, own_sem.at[3]),
        pltpu.make_async_copy(rts_ref.at[me_freq], rt_ref, own_sem.at[4]),
    )

    load(0).start()
    for table in tables:
        table.start()
    barrier = pltpu.get_barrier_semaphore()
    run(
        1,
        N_SHOT,
        lambda n: pl.semaphore_signal(
            barrier, 1, device_id=(shot_peer_of(me, me_freq, n), me_freq), device_id_type=MESH
        ),
    )
    for e in range(1, N_FREQ):
        pl.semaphore_signal(
            barrier, 1, device_id=(me, lax.rem(me_freq + e, N_FREQ)), device_id_type=MESH
        )
    pl.semaphore_wait(barrier, N_SHOT + N_FREQ - 2)

    def send_next(copy, n):
        copy(n - WINDOW).wait_send()
        copy(n).start()

    for n in range(1, WINDOW + 1):
        data_copy(n).start()
    own = pltpu.make_async_copy(rec_ref.at[:, pl.ds(me * FL, FL)], xb.at[me], own_sem.at[0])
    own.start()
    slot = lax.broadcasted_iota(jnp.int32, (4 * SD, R), 0)
    key = jnp.where(slot < SD, owners_ref[0] * SD + slot, owners_ref[1] * SD + slot - SD)
    key = jnp.where(slot < 2 * SD, key, owners_ref[2] * SD + slot - 2 * SD)
    key = jnp.where(slot < 3 * SD, key, -1)
    for b in range(SD // BLK):
        if b + 1 < SD // BLK:
            load(b + 1).start()
        load(b).wait()
        for ch in range(R // 128):
            part = block[b % 2, :, :, :, ch * 128 : (ch + 1) * 128]
            wide[ch] = part.astype(jnp.float32).reshape(rows * BLK, 128)

        def bin_shot(m, carry):
            data = jnp.concatenate(
                [wide[ch, pl.ds(m, rows, stride=BLK), :] for ch in range(R // 128)], axis=1
            ).astype(jnp.bfloat16)
            where = shot_ref[pl.ds(b * BLK + m, 1), :]
            one_hot = (jnp.broadcast_to(where, key.shape) == key).astype(jnp.bfloat16)
            out = lax.dot_general(
                data, one_hot, (((1,), (1,)), ((), ())), preferred_element_type=jnp.float32
            )
            real, imag = out[:freqs], out[freqs:]
            narrow[0, pl.ds(m, freqs, stride=BLK), :] = real[:, :128]
            narrow[1, pl.ds(m, freqs, stride=BLK), :] = real[:, 128:] + pltpu.roll(imag[:, 128:], SD, 1)
            narrow[2, pl.ds(m, freqs, stride=BLK), :] = imag[:, :128]
            due = b * BLK + m

            @pl.when((lax.rem(due, 2) == 0) & (due // 2 + WINDOW + 1 < N_SHOT))
            def _():
                send_next(data_copy, due // 2 + WINDOW + 1)

            return carry

        lax.fori_loop(0, BLK, bin_shot, 0)
        for ch in range(3):
            part = narrow[ch].reshape(freqs, BLK, 128).astype(jnp.bfloat16)
            coeffs[:, b * BLK : (b + 1) * BLK, ch * 128 : (ch + 1) * 128] = part
    kept = pltpu.make_async_copy(coeffs.at[pl.ds(me * FL, FL)], cb.at[me], own_sem.at[1])
    kept.start()

    def data_to_coeff(n):
        data_copy(N_SHOT - 1 - WINDOW + n).wait_send()
        coeff_copy(n).start()

    run(1, WINDOW + 1, data_to_coeff)
    run(WINDOW + 1, AHEAD, lambda n: coeff_copy(n).start())
    own.wait()
    kept.wait()
    run(1, N_SHOT, lambda n: data_copy(n).wait_recv())

    for j in range(FL):
        for t in range(STEPS):
            owner = owners_ref[t]
            real, imag = xb[owner, 0, j], xb[owner, 1, j]
            under = 3 if t == 2 else 4 + t
            top = slice(t * SD, (t + 1) * SD)
            low = slice(under * SD, (under + 1) * SD)
            w_ref[j, top, :R] = real
            w_ref[j, top, R:] = imag
            w_ref[j, low, :R] = -imag
            w_ref[j, low, R:] = real

    lane = lax.broadcasted_iota(jnp.int32, (GROUP * SD, 128), 1)

    def predict_group(g, carry):
        for i in range(GROUP):
            if i == 0:

                @pl.when(g > 0)
                def _():
                    coeff_copy(g * GROUP).wait_recv()
            else:
                coeff_copy(g * GROUP + i).wait_recv()

        @pl.when(AHEAD + g * GROUP < N_SHOT)
        def _():
            for i in range(GROUP):
                coeff_copy(AHEAD + g * GROUP + i).start()

        shots = [shot_source_of(me, me_freq, g * GROUP + i) for i in range(GROUP)]
        cols = jnp.zeros((GROUP * SD, 128), jnp.float32)
        for j in range(FL):
            lhs = jnp.concatenate([cb[s, j] for s in shots], axis=0)
            acc = jnp.dot(lhs, w_ref[j], preferred_element_type=jnp.float32)
            pred = (gain * acc).astype(jnp.bfloat16)
            pr, pi = pred[:, :R], pred[:, R:]
            for i, s in enumerate(shots):
                pb[s, 0, j] = pr[i * SD : (i + 1) * SD]
                pb[s, 1, j] = pi[i * SD : (i + 1) * SD]
            pr, pi = pr.astype(jnp.float32), pi.astype(jnp.float32)
            xr = jnp.concatenate([xb[s, 0, j] for s in shots], axis=0).astype(jnp.float32)
            xi = jnp.concatenate([xb[s, 1, j] for s in shots], axis=0).astype(jnp.float32)
            spec = jnp.sum(pr * pr + pi * pi, axis=1, keepdims=True)
            cr = jnp.sum(pr * xr + pi * xi, axis=1, keepdims=True)
            ci = jnp.sum(pr * xi - pi * xr, axis=1, keepdims=True)
            for q, col in enumerate((spec, cr, ci)):
                cols = jnp.where(lane == 3 * j + q, col, cols)
        flat = cols.T[:8]
        for i, s in enumerate(shots):
            pair = flat[:, (i // 2) * 128 : (i // 2) * 128 + 128]
            corr[s] = pair if i % 2 == 0 else pltpu.roll(pair, SD, 1)
        for i in range(GROUP):
            if i == 0:

                @pl.when(g > 0)
                def _():
                    corr_copy(g * GROUP).start()
            else:
                corr_copy(g * GROUP + i).start()
        return carry

    lax.fori_loop(0, N_SHOT // GROUP, predict_group, 0)
    arrived[me] = corr[me]
    run(1, N_SHOT, lambda n: corr_copy(n).wait_recv())

    for table in tables:
        table.wait()
    parts[me_freq] = jnp.dot(
        ct_ref[...],
        arrived[...].reshape(N_SHOT * 8, 128),
        precision=HIGH,
        preferred_element_type=jnp.float32,
    )
    for e in range(1, N_FREQ):
        part_copy(e).start()
    for e in range(1, N_FREQ):
        part_copy(e).wait()
    total = parts[0]
    for e in range(1, N_FREQ):
        total = total + parts[e]
    row64 = lax.broadcasted_iota(jnp.int32, (64, 128), 0)
    row = lax.broadcasted_iota(jnp.int32, (32, 128), 0)
    ext_ref[...] = total[:64] + jnp.where(row64 == TAPS - 1, damping, 0.0)
    rhs = total[64:] + jnp.where(row == HALF, damping, 0.0)
    cols = [ext_ref[pl.ds(TAPS - 1 - k, 32), :] for k in range(TAPS)]
    inverse = []
    for p in range(TAPS):
        inv = 1.0 / cols[p][p : p + 1, :]
        inverse.append(inv)
        if p == TAPS - 1:
            break
        factor = jnp.where(row > p, cols[p] * inv, 0.0)
        rhs = rhs - factor * rhs[p : p + 1, :]
        for k in range(p + 1, TAPS):
            cols[k] = cols[k] - factor * cols[k][p : p + 1, :]
    found = jnp.zeros((32, 128), jnp.float32)
    for p in range(TAPS - 1, -1, -1):
        value = rhs[p : p + 1, :] * inverse[p]
        found = jnp.where(row == p, value, found)
        rhs = rhs - cols[p] * value
    resp = jnp.dot(rt_ref[...], found, precision=HIGH, preferred_element_type=jnp.float32)
    answer[...] = resp.reshape(N_SHOT, 8, 128)
    run(1, N_SHOT, lambda n: resp_copy(n).start())
    resp_ref[me] = answer[me]
    filt_ref[...] = jnp.concatenate([found, jnp.zeros((96, 128), jnp.float32)], axis=0).T[:SD]
    run(1, N_SHOT, lambda n: resp_copy(n).wait_recv())

    diagonal = lax.broadcasted_iota(jnp.int32, (SD, 128), 0) == lax.broadcasted_iota(
        jnp.int32, (SD, 128), 1
    )

    def compute(n):
        shot, freq = any_peer_of(me, me_freq, n)
        resp = resp_ref[shot]
        part = pl.ds(pl.multiple_of(freq * width, width), width)

        def column(q):
            spread = jnp.broadcast_to(resp[q : q + 1], (SD, 128))
            return jnp.sum(jnp.where(diagonal, spread, 0.0), axis=1, keepdims=True)

        for j in range(FL):
            real, imag = column(j), column(FL + j)
            xr = xb[shot, 0, j, :, part].astype(jnp.float32)
            xi = xb[shot, 1, j, :, part].astype(jnp.float32)
            pr = pb[shot, 0, j, :, part].astype(jnp.float32)
            pi = pb[shot, 1, j, :, part].astype(jnp.float32)
            sb[n, 0, j] = (xr - (real * pr - imag * pi)).astype(jnp.bfloat16)
            sb[n, 1, j] = (xi - (real * pi + imag * pr)).astype(jnp.bfloat16)

    def residual_step(n):
        compute(n)
        residual_copy(n).start()

    run(1, N_DEV, residual_step)
    compute(0)
    stay = pltpu.make_async_copy(sb.at[0], out_ref.at[mine], own_sem.at[2])
    stay.start()
    stay.wait()
    run(1, N_SHOT, lambda n: coeff_copy(n).wait_send())
    run(1, N_SHOT, lambda n: corr_copy(n).wait_send())
    run(1, N_SHOT, lambda n: resp_copy(n).wait_send())
    run(1, N_DEV, lambda n: residual_copy(n).wait())


def fused(owners, recorded, rec_shot, ct, rt, damping, gain):
    freqs = recorded.shape[1]
    width = 2 * STEPS * SD
    anywhere = pl.BlockSpec(memory_space=pl.ANY)
    whole = pl.BlockSpec(memory_space=pltpu.VMEM)
    slab = (N_SHOT, 2, FL, SD, R)
    small = (N_SHOT, 8, 128)
    pairs = [N_SHOT, N_SHOT, N_SHOT, N_FREQ, N_SHOT, N_DEV]
    return pl.pallas_call(
        lambda *refs: fused_kernel(damping, gain, *refs),
        in_specs=[pl.BlockSpec(memory_space=pltpu.SMEM), anywhere, whole, anywhere, anywhere],
        out_specs=[anywhere, whole],
        out_shape=(
            jax.ShapeDtypeStruct((N_DEV, 2, FL, SD, R // N_FREQ), jnp.bfloat16),
            jax.ShapeDtypeStruct((SD, 128), jnp.float32),
        ),
        scratch_shapes=[
            pltpu.VMEM((2, 2, freqs, BLK, R), jnp.bfloat16),
            pltpu.VMEM((R // 128, 2 * freqs * BLK, 128), jnp.float32),
            pltpu.VMEM((3, freqs * BLK, 128), jnp.float32),
            pltpu.VMEM((freqs, SD, width), jnp.bfloat16),
            pltpu.VMEM(slab, jnp.bfloat16),
            pltpu.VMEM((N_SHOT, FL, SD, width), jnp.bfloat16),
            pltpu.VMEM(slab, jnp.bfloat16),
            pltpu.VMEM((FL, width, 2 * R), jnp.bfloat16),
            pltpu.VMEM(small, jnp.float32),
            pltpu.VMEM(small, jnp.float32),
            pltpu.VMEM((N_FREQ, 96, 128), jnp.float32),
            pltpu.VMEM(small, jnp.float32),
            pltpu.VMEM(small, jnp.float32),
            pltpu.VMEM((64, 128), jnp.float32),
            pltpu.VMEM((N_DEV, 2, FL, SD, R // N_FREQ), jnp.bfloat16),
            pltpu.VMEM(ct.shape[1:], jnp.float32),
            pltpu.VMEM(rt.shape[1:], jnp.float32),
            pltpu.SemaphoreType.DMA((2,)),
            pltpu.SemaphoreType.DMA((5,)),
        ]
        + [pltpu.SemaphoreType.DMA((count,)) for count in pairs for _ in range(2)],
        compiler_params=pltpu.CompilerParams(
            collective_id=0, has_side_effects=True, vmem_limit_bytes=LIMIT
        ),
        name="fused",
    )(owners, recorded, rec_shot, ct, rt)


def transform_kernel(r_ref, t_ref, *rest):
    out_ref, wide_ref = rest[-2:]
    k = r_ref.shape[0]
    s = r_ref.shape[1]
    wide_ref[...] = r_ref[...].astype(jnp.float32).reshape(k * s, 128)
    group = 8
    for m in range(0, s, group):
        rows = jnp.concatenate(
            [wide_ref[pl.ds(m + g, k, stride=s), :].T.astype(jnp.bfloat16) for g in range(group)], axis=0
        )
        out = jnp.dot(rows, t_ref[...], preferred_element_type=jnp.float32).astype(jnp.bfloat16)
        out_ref[m : m + group] = out.reshape(group, 128, 2 * F)


def transform(spectra, table, chunk, before):
    k, shots, recv = spectra.shape
    step = 8
    base = chunk * (shots // step)
    in_specs = [
        pl.BlockSpec((k, step, recv), lambda i: (0, i, 0)),
        pl.BlockSpec((k, 2 * F), lambda i: (0, 0)),
    ]
    args = [spectra, table]
    alias = {}
    if before is not None:
        in_specs.append(pl.BlockSpec(memory_space=pl.ANY))
        args.append(before)
        alias = {2: 0}
    return pl.pallas_call(
        transform_kernel,
        grid=(shots // step,),
        in_specs=in_specs,
        out_specs=pl.BlockSpec((step, recv, 2 * F), lambda i: (i + base, 0, 0)),
        out_shape=jax.ShapeDtypeStruct((SD, recv, 2 * F), jnp.bfloat16),
        scratch_shapes=[pltpu.VMEM((k * step, recv), jnp.float32)],
        input_output_aliases=alias,
        compiler_params=pltpu.CompilerParams(
            dimension_semantics=("arbitrary",), vmem_limit_bytes=LIMIT
        ),
        cost_estimate=pl.CostEstimate(flops=2 * 10**9, bytes_accessed=12 * 10**6, transcendentals=0),
        name=f"transform{chunk}",
    )(*args)


def per_device(recorded, rec_shot, owners):
    gain = (N_SHOT / (2.0 * R * STEPS)) ** 0.5
    ct, rt = jnp.asarray(corr_table()), jnp.asarray(resp_table())
    table = jnp.asarray(time_table(), dtype=jnp.bfloat16)
    res, filt = fused(owners, recorded, rec_shot, ct, rt, REG * R * F, gain)
    primaries = transform(res.reshape(2 * F, SD, R // N_FREQ), table, 0, None)
    return (primaries, filt[:, :TAPS])


def solution(mesh):
    placed = (P(None, "freq", "shot", None), P("shot", None), P())
    return jax.shard_map(
        per_device,
        mesh=mesh,
        in_specs=placed,
        out_specs=(P("shot", "freq", None), P("shot", None)),
        check_vma=False,
    )
```

```python
import math

import jax
import jax.numpy as jnp
import numpy as np
from jax import lax
from jax.experimental import pallas as pl
from jax.experimental.pallas import tpu as pltpu
from jax.sharding import PartitionSpec as P

F = 256
TAPS = 31
STEPS = 3
HALF = (TAPS - 1) // 2
REG = 2.0
N_SHOT = 32
N_FREQ = 4
N_DEV = N_SHOT * N_FREQ
FL = F // N_DEV
SD = 64
R = 512
BLK = 16
MIB = 1 << 20
LIMIT = 60 * MIB
GROUP = 4
AHEAD = 24
WINDOW = 12
HIGH = lax.Precision.HIGHEST
MESH = pl.DeviceIdType.MESH


def device_freqs():
    dev = np.arange(N_DEV)
    return (dev % N_FREQ)[:, None] * (F // N_FREQ) + (dev // N_FREQ)[:, None] * FL + np.arange(FL)[None, :]


def angle(freq, step):
    return ((freq * step) % (2 * F)).astype(np.float64) * (2.0 * math.pi / (2 * F))


def corr_table():
    freqs = device_freqs().reshape(N_SHOT, N_FREQ, FL)
    lags = np.abs(np.arange(64) - (TAPS - 1))
    taps = np.arange(32) - HALF
    table = np.zeros((N_FREQ, 96, N_SHOT, 8))
    for j in range(FL):
        col = freqs[:, :, j].T[:, None, :]
        table[:, :64, :, 3 * j] = np.cos(angle(col, lags[None, :, None]))
        table[:, 64:, :, 3 * j + 1] = np.cos(angle(col, taps[None, :, None]))
        table[:, 64:, :, 3 * j + 2] = -np.sin(angle(col, taps[None, :, None]))
    return table.reshape(N_FREQ, 96, N_SHOT * 8).astype(np.float32)


def resp_table():
    freqs = device_freqs().reshape(N_SHOT, N_FREQ, FL)
    taps = np.arange(32) - HALF
    valid = np.arange(32) < TAPS
    table = np.zeros((N_FREQ, N_SHOT, 8, 32))
    for j in range(FL):
        ang = angle(freqs[:, :, j].T[:, :, None], taps[None, None, :])
        table[:, :, j] = np.cos(ang) * valid
        table[:, :, FL + j] = -np.sin(ang) * valid
    return table.reshape(N_FREQ, N_SHOT * 8, 32).astype(np.float32)


def time_table():
    freqs = device_freqs()
    ang = angle(freqs[:, :, None], np.arange(2 * F)[None, None, :])
    norm = 1.0 / math.sqrt(F)
    table = np.stack([np.cos(ang) * norm, -np.sin(ang) * norm], axis=1)
    return table.reshape(2 * F, 2 * F).astype(np.float32)


def turned(back, offset, size):
    return jnp.where(back == 1, lax.rem(size - offset, size), offset)


def shot_at(me, d, back):
    x = lax.rem(me // 16 + d // 16, 2)
    z = lax.rem(lax.rem(me // 4, 4) + turned(back, lax.rem(d // 4, 4), 4), 4)
    y = lax.rem(lax.rem(me, 4) + turned(back, lax.rem(d, 4), 4), 4)
    return x * 16 + z * 4 + y


def shot_peer_of(me, me_freq, n):
    return shot_at(me, lax.rem(n * 11, N_SHOT), lax.rem(me_freq, 2))


def shot_source_of(me, me_freq, n):
    return shot_at(me, lax.rem(n * 11, N_SHOT), 1 - lax.rem(me_freq, 2))


def any_peer_of(me, me_freq, n):
    core = lax.rem(me_freq, 2)
    d = lax.rem(n * 43, N_DEV)
    x = lax.rem((me_freq // 2) * 2 + me // 16 + turned(core, lax.rem(d // 16, 4), 4), 4)
    z = lax.rem(lax.rem(me // 4, 4) + turned(core, lax.rem(d // 4, 4), 4), 4)
    y = lax.rem(lax.rem(me, 4) + turned(core, lax.rem(d, 4), 4), 4)
    other = lax.rem(core + d // 64, 2)
    return lax.rem(x, 2) * 16 + z * 4 + y, (x // 2) * 2 + other


def fused_kernel(
    damping, gain,
    owners_ref, rec_ref, shot_ref, cts_ref, rts_ref,
    out_ref, filt_ref,
    block, wide, narrow, coeffs, xb, cb, pb, w_ref, corr, arrived, parts, answer, resp_ref, ext_ref, sb, ct_ref, rt_ref,
    load_sem, own_sem, dsend, drecv, csend, crecv, qsend, qrecv, fsend, frecv, rsend, rrecv, send_sem, recv_sem,
):
    me = lax.axis_index("shot")
    me_freq = lax.axis_index("freq")
    mine = me * N_FREQ + me_freq
    freqs = rec_ref.shape[1]
    rows = 2 * freqs
    width = R // N_FREQ

    def remote(src, dst, send, recv, device):
        return pltpu.make_async_remote_copy(
            src_ref=src, dst_ref=dst, send_sem=send, recv_sem=recv, device_id=device, device_id_type=MESH
        )

    def data_copy(n):
        peer = shot_peer_of(me, me_freq, n)
        return remote(
            rec_ref.at[:, pl.ds(peer * FL, FL)], xb.at[me], dsend.at[n], drecv.at[n], (peer, me_freq)
        )

    def coeff_copy(n):
        peer = shot_peer_of(me, me_freq, n)
        return remote(
            coeffs.at[pl.ds(peer * FL, FL)], cb.at[me], csend.at[n], crecv.at[n], (peer, me_freq)
        )

    def corr_copy(n):
        peer = shot_source_of(me, me_freq, n)
        return remote(corr.at[peer], arrived.at[me], qsend.at[n], qrecv.at[n], (peer, me_freq))

    def part_copy(e):
        other = lax.rem(me_freq + e, N_FREQ)
        return remote(parts.at[me_freq], parts.at[me_freq], fsend.at[e], frecv.at[e], (me, other))

    def resp_copy(n):
        peer = shot_peer_of(me, me_freq, n)
        return remote(answer.at[peer], resp_ref.at[me], rsend.at[n], rrecv.at[n], (peer, me_freq))

    def residual_copy(n):
        return remote(
            sb.at[n], out_ref.at[mine], send_sem.at[n], recv_sem.at[n], any_peer_of(me, me_freq, n)
        )

    def run(first, last, action):
        def step(n, carry):
            action(n)
            return carry

        lax.fori_loop(first, last, step, 0)

    def load(b):
        return pltpu.make_async_copy(
            rec_ref.at[:, :, pl.ds(b * BLK, BLK), :], block.at[b % 2], load_sem.at[b % 2]
        )

    tables = (
        pltpu.make_async_copy(cts_ref.at[me_freq], ct_ref, own_sem.at[3]),
        pltpu.make_async_copy(rts_ref.at[me_freq], rt_ref, own_sem.at[4]),
    )

    load(0).start()
    for table in tables:
        table.start()
    barrier = pltpu.get_barrier_semaphore()
    run(
        1,
        N_SHOT,
        lambda n: pl.semaphore_signal(
            barrier, 1, device_id=(shot_peer_of(me, me_freq, n), me_freq), device_id_type=MESH
        ),
    )
    for e in range(1, N_FREQ):
        pl.semaphore_signal(
            barrier, 1, device_id=(me, lax.rem(me_freq + e, N_FREQ)), device_id_type=MESH
        )
    pl.semaphore_wait(barrier, N_SHOT + N_FREQ - 2)

    def send_next(copy, n):
        copy(n - WINDOW).wait_send()
        copy(n).start()

    for n in range(1, WINDOW + 1):
        data_copy(n).start()
    own = pltpu.make_async_copy(rec_ref.at[:, pl.ds(me * FL, FL)], xb.at[me], own_sem.at[0])
    own.start()
    slot = lax.broadcasted_iota(jnp.int32, (4 * SD, R), 0)
    key = jnp.where(slot < SD, owners_ref[0] * SD + slot, owners_ref[1] * SD + slot - SD)
    key = jnp.where(slot < 2 * SD, key, owners_ref[2] * SD + slot - 2 * SD)
    key = jnp.where(slot < 3 * SD, key, -1)
    for b in range(SD // BLK):
        if b + 1 < SD // BLK:
            load(b + 1).start()
        load(b).wait()
        for ch in range(R // 128):
            part = block[b % 2, :, :, :, ch * 128 : (ch + 1) * 128]
            wide[ch] = part.astype(jnp.float32).reshape(rows * BLK, 128)

        def bin_shot(m, carry):
            data = jnp.concatenate(
                [wide[ch, pl.ds(m, rows, stride=BLK), :] for ch in range(R // 128)], axis=1
            ).astype(jnp.bfloat16)
            where = shot_ref[pl.ds(b * BLK + m, 1), :]
            one_hot = (jnp.broadcast_to(where, key.shape) == key).astype(jnp.bfloat16)
            out = lax.dot_general(
                data, one_hot, (((1,), (1,)), ((), ())), preferred_element_type=jnp.float32
            )
            real, imag = out[:freqs], out[freqs:]
            narrow[0, pl.ds(m, freqs, stride=BLK), :] = real[:, :128]
            narrow[1, pl.ds(m, freqs, stride=BLK), :] = real[:, 128:] + pltpu.roll(imag[:, 128:], SD, 1)
            narrow[2, pl.ds(m, freqs, stride=BLK), :] = imag[:, :128]
            due = b * BLK + m

            @pl.when((lax.rem(due, 2) == 0) & (due // 2 + WINDOW + 1 < N_SHOT))
            def _():
                send_next(data_copy, due // 2 + WINDOW + 1)

            return carry

        lax.fori_loop(0, BLK, bin_shot, 0)
        for ch in range(3):
            part = narrow[ch].reshape(freqs, BLK, 128).astype(jnp.bfloat16)
            coeffs[:, b * BLK : (b + 1) * BLK, ch * 128 : (ch + 1) * 128] = part
    kept = pltpu.make_async_copy(coeffs.at[pl.ds(me * FL, FL)], cb.at[me], own_sem.at[1])
    kept.start()

    def data_to_coeff(n):
        data_copy(N_SHOT - 1 - WINDOW + n).wait_send()
        coeff_copy(n).start()

    run(1, WINDOW + 1, data_to_coeff)
    run(WINDOW + 1, AHEAD, lambda n: coeff_copy(n).start())
    own.wait()
    kept.wait()
    run(1, N_SHOT, lambda n: data_copy(n).wait_recv())

    for j in range(FL):
        for t in range(STEPS):
            owner = owners_ref[t]
            real, imag = xb[owner, 0, j], xb[owner, 1, j]
            under = 3 if t == 2 else 4 + t
            top = slice(t * SD, (t + 1) * SD)
            low = slice(under * SD, (under + 1) * SD)
            w_ref[j, top, :R] = real
            w_ref[j, top, R:] = imag
            w_ref[j, low, :R] = -imag
            w_ref[j, low, R:] = real

    lane = lax.broadcasted_iota(jnp.int32, (GROUP * SD, 128), 1)

    def predict_group(g, carry):
        for i in range(GROUP):
            if i == 0:

                @pl.when(g > 0)
                def _():
                    coeff_copy(g * GROUP).wait_recv()
            else:
                coeff_copy(g * GROUP + i).wait_recv()

        @pl.when(AHEAD + g * GROUP < N_SHOT)
        def _():
            for i in range(GROUP):
                coeff_copy(AHEAD + g * GROUP + i).start()

        shots = [shot_source_of(me, me_freq, g * GROUP + i) for i in range(GROUP)]
        cols = jnp.zeros((GROUP * SD, 128), jnp.float32)
        for j in range(FL):
            lhs = jnp.concatenate([cb[s, j] for s in shots], axis=0)
            acc = jnp.dot(lhs, w_ref[j], preferred_element_type=jnp.float32)
            pred = (gain * acc).astype(jnp.bfloat16)
            pr, pi = pred[:, :R], pred[:, R:]
            for i, s in enumerate(shots):
                pb[s, 0, j] = pr[i * SD : (i + 1) * SD]
                pb[s, 1, j] = pi[i * SD : (i + 1) * SD]
            pr, pi = pr.astype(jnp.float32), pi.astype(jnp.float32)
            xr = jnp.concatenate([xb[s, 0, j] for s in shots], axis=0).astype(jnp.float32)
            xi = jnp.concatenate([xb[s, 1, j] for s in shots], axis=0).astype(jnp.float32)
            spec = jnp.sum(pr * pr + pi * pi, axis=1, keepdims=True)
            cr = jnp.sum(pr * xr + pi * xi, axis=1, keepdims=True)
            ci = jnp.sum(pr * xi - pi * xr, axis=1, keepdims=True)
            for q, col in enumerate((spec, cr, ci)):
                cols = jnp.where(lane == 3 * j + q, col, cols)
        flat = cols.T[:8]
        for i, s in enumerate(shots):
            pair = flat[:, (i // 2) * 128 : (i // 2) * 128 + 128]
            corr[s] = pair if i % 2 == 0 else pltpu.roll(pair, SD, 1)
        for i in range(GROUP):
            if i == 0:

                @pl.when(g > 0)
                def _():
                    corr_copy(g * GROUP).start()
            else:
                corr_copy(g * GROUP + i).start()
        return carry

    lax.fori_loop(0, N_SHOT // GROUP, predict_group, 0)
    arrived[me] = corr[me]
    run(1, N_SHOT, lambda n: corr_copy(n).wait_recv())

    for table in tables:
        table.wait()
    parts[me_freq] = jnp.dot(
        ct_ref[...],
        arrived[...].reshape(N_SHOT * 8, 128),
        precision=HIGH,
        preferred_element_type=jnp.float32,
    )
    for e in range(1, N_FREQ):
        part_copy(e).start()
    for e in range(1, N_FREQ):
        part_copy(e).wait()
    total = parts[0]
    for e in range(1, N_FREQ):
        total = total + parts[e]
    row64 = lax.broadcasted_iota(jnp.int32, (64, 128), 0)
    row = lax.broadcasted_iota(jnp.int32, (32, 128), 0)
    ext_ref[...] = total[:64] + jnp.where(row64 == TAPS - 1, damping, 0.0)
    rhs = total[64:] + jnp.where(row == HALF, damping, 0.0)
    cols = [ext_ref[pl.ds(TAPS - 1 - k, 32), :] for k in range(TAPS)]
    inverse = []
    for p in range(TAPS):
        inv = 1.0 / cols[p][p : p + 1, :]
        inverse.append(inv)
        if p == TAPS - 1:
            break
        factor = jnp.where(row > p, cols[p] * inv, 0.0)
        rhs = rhs - factor * rhs[p : p + 1, :]
        for k in range(p + 1, TAPS):
            cols[k] = cols[k] - factor * cols[k][p : p + 1, :]
    found = jnp.zeros((32, 128), jnp.float32)
    for p in range(TAPS - 1, -1, -1):
        value = rhs[p : p + 1, :] * inverse[p]
        found = jnp.where(row == p, value, found)
        rhs = rhs - cols[p] * value
    resp = jnp.dot(rt_ref[...], found, precision=HIGH, preferred_element_type=jnp.float32)
    answer[...] = resp.reshape(N_SHOT, 8, 128)
    run(1, N_SHOT, lambda n: resp_copy(n).start())
    resp_ref[me] = answer[me]
    filt_ref[...] = jnp.concatenate([found, jnp.zeros((96, 128), jnp.float32)], axis=0).T[:SD]
    run(1, N_SHOT, lambda n: resp_copy(n).wait_recv())

    diagonal = lax.broadcasted_iota(jnp.int32, (SD, 128), 0) == lax.broadcasted_iota(
        jnp.int32, (SD, 128), 1
    )

    def compute(n):
        shot, freq = any_peer_of(me, me_freq, n)
        resp = resp_ref[shot]
        part = pl.ds(pl.multiple_of(freq * width, width), width)

        def column(q):
            spread = jnp.broadcast_to(resp[q : q + 1], (SD, 128))
            return jnp.sum(jnp.where(diagonal, spread, 0.0), axis=1, keepdims=True)

        for j in range(FL):
            real, imag = column(j), column(FL + j)
            xr = xb[shot, 0, j, :, part].astype(jnp.float32)
            xi = xb[shot, 1, j, :, part].astype(jnp.float32)
            pr = pb[shot, 0, j, :, part].astype(jnp.float32)
            pi = pb[shot, 1, j, :, part].astype(jnp.float32)
            sb[n, 0, j] = (xr - (real * pr - imag * pi)).astype(jnp.bfloat16)
            sb[n, 1, j] = (xi - (real * pi + imag * pr)).astype(jnp.bfloat16)

    def residual_step(n):
        compute(n)
        residual_copy(n).start()

    run(1, N_DEV, residual_step)
    compute(0)
    stay = pltpu.make_async_copy(sb.at[0], out_ref.at[mine], own_sem.at[2])
    stay.start()
    stay.wait()
    run(1, N_SHOT, lambda n: coeff_copy(n).wait_send())
    run(1, N_SHOT, lambda n: corr_copy(n).wait_send())
    run(1, N_SHOT, lambda n: resp_copy(n).wait_send())
    run(1, N_DEV, lambda n: residual_copy(n).wait())


def fused(owners, recorded, rec_shot, ct, rt, damping, gain):
    freqs = recorded.shape[1]
    width = 2 * STEPS * SD
    anywhere = pl.BlockSpec(memory_space=pl.ANY)
    whole = pl.BlockSpec(memory_space=pltpu.VMEM)
    slab = (N_SHOT, 2, FL, SD, R)
    small = (N_SHOT, 8, 128)
    pairs = [N_SHOT, N_SHOT, N_SHOT, N_FREQ, N_SHOT, N_DEV]
    return pl.pallas_call(
        lambda *refs: fused_kernel(damping, gain, *refs),
        in_specs=[pl.BlockSpec(memory_space=pltpu.SMEM), anywhere, whole, anywhere, anywhere],
        out_specs=[anywhere, whole],
        out_shape=(
            jax.ShapeDtypeStruct((N_DEV, 2, FL, SD, R // N_FREQ), jnp.bfloat16),
            jax.ShapeDtypeStruct((SD, 128), jnp.float32),
        ),
        scratch_shapes=[
            pltpu.VMEM((2, 2, freqs, BLK, R), jnp.bfloat16),
            pltpu.VMEM((R // 128, 2 * freqs * BLK, 128), jnp.float32),
            pltpu.VMEM((3, freqs * BLK, 128), jnp.float32),
            pltpu.VMEM((freqs, SD, width), jnp.bfloat16),
            pltpu.VMEM(slab, jnp.bfloat16),
            pltpu.VMEM((N_SHOT, FL, SD, width), jnp.bfloat16),
            pltpu.VMEM(slab, jnp.bfloat16),
            pltpu.VMEM((FL, width, 2 * R), jnp.bfloat16),
            pltpu.VMEM(small, jnp.float32),
            pltpu.VMEM(small, jnp.float32),
            pltpu.VMEM((N_FREQ, 96, 128), jnp.float32),
            pltpu.VMEM(small, jnp.float32),
            pltpu.VMEM(small, jnp.float32),
            pltpu.VMEM((64, 128), jnp.float32),
            pltpu.VMEM((N_DEV, 2, FL, SD, R // N_FREQ), jnp.bfloat16),
            pltpu.VMEM(ct.shape[1:], jnp.float32),
            pltpu.VMEM(rt.shape[1:], jnp.float32),
            pltpu.SemaphoreType.DMA((2,)),
            pltpu.SemaphoreType.DMA((5,)),
        ]
        + [pltpu.SemaphoreType.DMA((count,)) for count in pairs for _ in range(2)],
        compiler_params=pltpu.CompilerParams(
            collective_id=0, has_side_effects=True, vmem_limit_bytes=LIMIT
        ),
        name="fused",
    )(owners, recorded, rec_shot, ct, rt)


def transform_kernel(r_ref, t_ref, *rest):
    out_ref, wide_ref = rest[-2:]
    k = r_ref.shape[0]
    s = r_ref.shape[1]
    wide_ref[...] = r_ref[...].astype(jnp.float32).reshape(k * s, 128)
    group = 8
    for m in range(0, s, group):
        rows = jnp.concatenate(
            [wide_ref[pl.ds(m + g, k, stride=s), :].T.astype(jnp.bfloat16) for g in range(group)], axis=0
        )
        out = jnp.dot(rows, t_ref[...], preferred_element_type=jnp.float32).astype(jnp.bfloat16)
        out_ref[m : m + group] = out.reshape(group, 128, 2 * F)


def transform(spectra, table, chunk, before):
    k, shots, recv = spectra.shape
    step = 8
    base = chunk * (shots // step)
    in_specs = [
        pl.BlockSpec((k, step, recv), lambda i: (0, i, 0)),
        pl.BlockSpec((k, 2 * F), lambda i: (0, 0)),
    ]
    args = [spectra, table]
    alias = {}
    if before is not None:
        in_specs.append(pl.BlockSpec(memory_space=pl.ANY))
        args.append(before)
        alias = {2: 0}
    return pl.pallas_call(
        transform_kernel,
        grid=(shots // step,),
        in_specs=in_specs,
        out_specs=pl.BlockSpec((step, recv, 2 * F), lambda i: (i + base, 0, 0)),
        out_shape=jax.ShapeDtypeStruct((SD, recv, 2 * F), jnp.bfloat16),
        scratch_shapes=[pltpu.VMEM((k * step, recv), jnp.float32)],
        input_output_aliases=alias,
        compiler_params=pltpu.CompilerParams(
            dimension_semantics=("arbitrary",), vmem_limit_bytes=LIMIT
        ),
        cost_estimate=pl.CostEstimate(flops=2 * 10**9, bytes_accessed=12 * 10**6, transcendentals=0),
        name=f"transform{chunk}",
    )(*args)


def per_device(recorded, rec_shot, owners):
    gain = (N_SHOT / (2.0 * R * STEPS)) ** 0.5
    ct, rt = jnp.asarray(corr_table()), jnp.asarray(resp_table())
    table = jnp.asarray(time_table(), dtype=jnp.bfloat16)
    res, filt = fused(owners, recorded, rec_shot, ct, rt, REG * R * F, gain)
    primaries = transform(res.reshape(2 * F, SD, R // N_FREQ), table, 0, None)
    return (primaries, filt[:, :TAPS])


def solution(mesh):
    placed = (P(None, "freq", "shot", None), P("shot", None), P())
    return jax.shard_map(
        per_device,
        mesh=mesh,
        in_specs=placed,
        out_specs=(P("shot", "freq", None), P("shot", None)),
        check_vma=False,
    )
```
